256 devices in a mesh: rep: 16 (over x, y_hi, core), hid: 16 (over y_lo, z).
Axes of the slice: x: 4, y: 4 (y_hi: 2, y_lo: 2; y = y_hi * 2 + y_lo), z: 8, core: 2. Of those that a mesh axis runs over, the one named last changes fastest.
Arguments:
- tokens: bfloat16 [2, 8192, 1152], P(None, ('rep', 'hid')), may hold values from -6 to 6
- targets: bfloat16 [2, 8192, 1152], P(None, ('rep', 'hid')), may hold values from -6 to 6
- w_gate: float32 [16, 6912, 1152], P('rep', 'hid'), may hold values from -6 to 6
- w_up: float32 [16, 6912, 1152], P('rep', 'hid'), may hold values from -6 to 6
- w_down: float32 [16, 6912, 1152], P('rep', 'hid'), may hold values from -6 to 6
Outputs:
- new_gate: float32 [16, 6912, 1152], P('rep', 'hid')
- new_up: float32 [16, 6912, 1152], P('rep', 'hid')
- new_down: float32 [16, 6912, 1152], P('rep', 'hid')
The draws below stay inside these ranges and needn't reach their ends.
All inputs are finite; a program needn't handle non-finite values.
Results may differ from the reference program's by a relative error of at most 0.0086.
Values may be sent and summed in bfloat16 or wider, within the bound.
No kernel may reach another device: no remote copies, remote signals or barrier semaphores. Data moves between devices by JAX's collectives and lax.ppermute only.
A program may use at most 128 MiB of HBM per device.

```python
import jax
import jax.numpy as jnp
from jax import lax

D = 1152
FF = 6912
TOK_DEV = 32
STEPS = 2
TOKENS = 8192
REPLICAS = 16
N_REP = 16
N_HID = 16


def levels(rng, extent, shards, least, top_value):
    def one(position, parts):
        draws = jax.random.uniform(jax.random.fold_in(jax.random.fold_in(rng, 6), position), (parts,), jnp.float32, least / len(shards), top_value / len(shards))
        return jnp.repeat(jnp.exp(draws), extent[position] // parts).reshape((-1,) + (1,) * (len(extent) - position - 1))

    loudness = one(*shards[0])
    for cut in shards[1:]:
        loudness = loudness * one(*cut)
    return loudness


def scatter_about(key, shape, width, most, pieces=(), kind=jnp.bfloat16):
    entries = jax.random.normal(key, shape, jnp.float32) * width
    if len(pieces) > 0:
        entries = levels(key, shape, pieces, -0.22, 0.18) * entries
    return jnp.clip(entries, min=-most, max=most).astype(kind)


def setup_inputs(seed: int = 0) -> dict:
    streams_of = jax.random.split(jax.random.key(seed), 6)
    return {
        "tokens": scatter_about(streams_of[0], (STEPS, TOKENS, D), 1.0, 6.0, ((1, 256),)),
        "targets": scatter_about(streams_of[1], (STEPS, TOKENS, D), 1.0, 6.0, ((1, 256),)),
        "w_gate": scatter_about(streams_of[2], (REPLICAS, FF, D), 1.0, 6.0, ((0, 16), (1, 16)), jnp.float32),
        "w_up": scatter_about(streams_of[3], (REPLICAS, FF, D), 1.0, 6.0, ((0, 16), (1, 16)), jnp.float32),
        "w_down": scatter_about(streams_of[4], (REPLICAS, FF, D), 1.0, 6.0, ((0, 16), (1, 16)), jnp.float32),
    }


LEARNING_RATE = 0.5

def gelu_tanh(value):
    return jax.nn.gelu(value, approximate=True)

def contract_cols(left, right):
    return lax.dot_general(left, right, (((1,), (1,)), ((), ())), preferred_element_type=jnp.float32)

def contract_rows(left, right):
    return lax.dot_general(left, right, (((0,), (0,)), ((), ())), preferred_element_type=jnp.float32)

def replica_update(packed):
    gate_weight, up_weight, down_weight, token_batch, target_rows = packed
    scale_model = float(D) ** (-0.5)
    scale_hidden = float(FF) ** (-0.5)
    gate_half = gate_weight.astype(jnp.bfloat16)
    up_half = up_weight.astype(jnp.bfloat16)
    down_half = down_weight.astype(jnp.bfloat16)
    gate_value = contract_cols(token_batch, gate_half) * scale_model
    up_value = contract_cols(token_batch, up_half) * scale_model
    activated, gelu_back = jax.vjp(gelu_tanh, gate_value)
    hidden = (activated * up_value).astype(jnp.bfloat16)
    output = jnp.dot(hidden, down_half, preferred_element_type=jnp.float32) * scale_hidden
    residual = (output - target_rows.astype(jnp.float32)).astype(jnp.bfloat16)
    grad_down = contract_rows(hidden, residual) * scale_hidden
    hidden_grad = contract_cols(residual, down_half) * scale_hidden
    gate_grad = gelu_back(hidden_grad * up_value)[0].astype(jnp.bfloat16)
    up_grad = (hidden_grad * activated).astype(jnp.bfloat16)
    grad_gate = contract_rows(gate_grad, token_batch) * scale_model
    grad_up = contract_rows(up_grad, token_batch) * scale_model
    return (gate_weight - LEARNING_RATE * grad_gate, up_weight - LEARNING_RATE * grad_up, down_weight - LEARNING_RATE * grad_down)

def average_pairs(weight, stride):
    grouped = weight.reshape(N_REP // (2 * stride), 2, stride, FF, D)
    averaged = (grouped[:, 0] + grouped[:, 1]) * 0.5
    return jnp.stack([averaged, averaged], axis=1).reshape(N_REP, FF, D)

def reference(tokens, targets, w_gate, w_up, w_down):
    weights = (w_gate, w_up, w_down)
    for step_index in range(STEPS):
        token_batch = tokens[step_index].reshape(N_REP, TOK_DEV * N_HID, D)
        target_rows = targets[step_index].reshape(N_REP, TOK_DEV * N_HID, D)
        stepped = lax.map(replica_update, weights + (token_batch, target_rows))
        weights = tuple((average_pairs(weight, 2 ** step_index) for weight in stepped))
    return (weights[0], weights[1], weights[2])
```

```python
import jax
import jax.numpy as jnp
from jax import lax
from jax.sharding import PartitionSpec as P

LEARNING_RATE = 0.5
BF16, F32 = jnp.bfloat16, jnp.float32


def gelu_tanh(value):
    return jax.nn.gelu(value, approximate=True)


def contract_cols(left, right):
    return lax.dot_general(left, right, (((1,), (1,)), ((), ())), preferred_element_type=F32)


def contract_rows(left, right):
    return lax.dot_general(left, right, (((0,), (0,)), ((), ())), preferred_element_type=F32)


def local(tokens, targets, w_gate, w_up, w_down, *, n_rep, n_z, hidden_units):
    n_hid = 2 * n_z
    rows, width = tokens.shape[1], tokens.shape[2]
    pair = 2 * rows
    scale_model = float(width) ** (-0.5)
    scale_hidden = float(hidden_units) ** (-0.5)

    def along_z(value, shift):
        pairs = [(h, (h // n_z) * n_z + (h % n_z + shift) % n_z) for h in range(n_hid)]
        return lax.ppermute(value, "hid", pairs)

    def across_y(value):
        return lax.ppermute(value, "hid", [(h, h ^ n_z) for h in range(n_hid)])

    def with_replica(value, mask):
        return lax.ppermute(value, "rep", [(r, r ^ mask) for r in range(n_rep)])

    order = (n_z // 2,) + tuple(k for d in range(n_z // 2 - 1, 0, -1) for k in (d, n_z - d))

    def gather_z(block):
        got = {k: along_z(block, -k) for k in order}
        return jnp.concatenate([block] + [got[k] for k in range(1, n_z)], axis=0)

    def reduce_z(partial):
        got = [along_z(partial[k * pair : (k + 1) * pair], k) for k in order]
        total = partial[:pair].astype(F32)
        for value in got:
            total = total + value.astype(F32)
        other = across_y(total.astype(BF16)).astype(F32)
        return total + jnp.concatenate([other[rows:], other[:rows]], axis=0)

    def forward(x, weights):
        gate = contract_cols(x, weights[0]) * scale_model
        up = contract_cols(x, weights[1]) * scale_model
        hidden = (gelu_tanh(gate) * up).astype(BF16)
        return gate, up, hidden

    def backward(x, residual, down_half, gate, up, hidden):
        activated, gelu_back = jax.vjp(gelu_tanh, gate)
        grad_down = contract_rows(hidden, residual) * scale_hidden
        hidden_grad = contract_cols(residual, down_half) * scale_hidden
        gate_grad = gelu_back(hidden_grad * up)[0].astype(BF16)
        up_grad = (hidden_grad * activated).astype(BF16)
        grad_gate = contract_rows(gate_grad, x) * scale_model
        grad_up = contract_rows(up_grad, x) * scale_model
        return grad_gate, grad_up, grad_down

    def residual_of(hidden, down_half, target):
        partial = jnp.dot(hidden, down_half, preferred_element_type=F32).astype(BF16)
        output = reduce_z(partial) * scale_hidden
        return (output - target.astype(F32)).astype(BF16)

    first = jnp.concatenate([tokens[0], across_y(tokens[0])], axis=0)
    x0 = gather_z(first)
    rest = jnp.concatenate([tokens[1], targets[0], targets[1]], axis=0)
    other = across_y(rest)
    second, target0, target1 = (
        jnp.concatenate([rest[i * rows : (i + 1) * rows], other[i * rows : (i + 1) * rows]], axis=0)
        for i in range(3)
    )

    weights = (w_gate[0], w_up[0], w_down[0])
    near = tuple(with_replica(w, 1) for w in weights)

    halves = tuple(w.astype(BF16) for w in weights)
    gate, up, hidden = forward(x0, halves)
    residual = gather_z(residual_of(hidden, halves[2], target0))
    grads = tuple(g.astype(BF16) for g in backward(x0, residual, halves[2], gate, up, hidden))
    near_grads = tuple(with_replica(g, 1) for g in grads)
    weights = tuple(
        (mine + theirs) * 0.5 - (LEARNING_RATE * 0.5) * (g.astype(F32) + n.astype(F32))
        for mine, theirs, g, n in zip(weights, near, grads, near_grads)
    )
    halves = tuple(w.astype(BF16) for w in weights)

    x1 = gather_z(second)
    x1_far = with_replica(x1, 2)
    core = lax.axis_index("rep") % 2
    units = w_gate.shape[1]
    cut = units // 2
    mine = jnp.stack([jnp.where(core == 0, w[:cut], w[cut:]) for w in halves])
    theirs = with_replica(mine, 2)
    beside = with_replica(theirs, 1)
    low = jnp.where(core == 0, theirs, beside)
    high = jnp.where(core == 0, beside, theirs)
    far = tuple(jnp.concatenate([low[i], high[i]], axis=0) for i in range(3))

    gate, up, hidden = forward(x1, halves)
    residual = gather_z(residual_of(hidden, halves[2], target1))
    residual_far = with_replica(residual, 2)
    grads = backward(x1, residual, halves[2], gate, up, hidden)
    gate, up, hidden = forward(x1_far, far)
    far_grads = backward(x1_far, residual_far, far[2], gate, up, hidden)
    result = tuple(
        (w + f.astype(F32)) * 0.5 - (LEARNING_RATE * 0.5) * (g + h)
        for w, f, g, h in zip(weights, far, grads, far_grads)
    )
    return tuple(w[None] for w in result)


def solution(mesh):
    n_rep, n_hid = mesh.shape["rep"], mesh.shape["hid"]
    hid_spec = P("rep", "hid", None)
    token_spec = P(None, ("rep", "hid"), None)

    def whole(tokens, targets, w_gate, w_up, w_down):
        def body(*args):
            return local(*args, n_rep=n_rep, n_z=n_hid // 2, hidden_units=w_gate.shape[1])

        return jax.shard_map(
            body,
            mesh=mesh,
            in_specs=(token_spec, token_spec, hid_spec, hid_spec, hid_spec),
            out_specs=(hid_spec, hid_spec, hid_spec),
            check_vma=False,
        )(tokens, targets, w_gate, w_up, w_down)

    return whole
```

```python
import jax
import jax.numpy as jnp
from jax import lax
from jax.sharding import PartitionSpec as P

LEARNING_RATE = 0.5
BF16, F32 = jnp.bfloat16, jnp.float32


def gelu_tanh(value):
    return jax.nn.gelu(value, approximate=True)


def contract_cols(left, right):
    return lax.dot_general(left, right, (((1,), (1,)), ((), ())), preferred_element_type=F32)


def contract_rows(left, right):
    return lax.dot_general(left, right, (((0,), (0,)), ((), ())), preferred_element_type=F32)


def local(tokens, targets, w_gate, w_up, w_down, *, n_rep, n_z, hidden_units):
    n_hid = 2 * n_z
    rows, width = tokens.shape[1], tokens.shape[2]
    pair = 2 * rows
    scale_model = float(width) ** (-0.5)
    scale_hidden = float(hidden_units) ** (-0.5)

    def along_z(value, shift):
        pairs = [(h, (h // n_z) * n_z + (h % n_z + shift) % n_z) for h in range(n_hid)]
        return lax.ppermute(value, "hid", pairs)

    def across_y(value):
        return lax.ppermute(value, "hid", [(h, h ^ n_z) for h in range(n_hid)])

    def with_replica(value, mask):
        return lax.ppermute(value, "rep", [(r, r ^ mask) for r in range(n_rep)])

    core = lax.axis_index("rep") % 2
    quarter = n_z // 4

    def opposite(value):
        pairs = []
        for r in range(n_rep):
            step = quarter if r % 2 == 0 else -quarter
            for h in range(n_hid):
                to = (h // n_z) * n_z + (h % n_z + step) % n_z
                pairs.append((r * n_hid + h, r * n_hid + to))
        return lax.ppermute(value, ("rep", "hid"), pairs)

    def gather_z(block):
        size = block.shape[0]
        below, above = along_z(block, 2), along_z(block, -2)
        both = jnp.concatenate([below, above], axis=0)
        left, right = along_z(both, 1), along_z(both, -1)
        across = opposite(jnp.where(core == 0, below, above))
        return jnp.concatenate(
            [block, left[size:], above, right[size:], across, left[:size], below, right[:size]], axis=0
        )

    def reduce_z(partial):
        part = [partial[k * pair : (k + 1) * pair] for k in range(n_z)]
        left = along_z(jnp.concatenate([part[3], part[7]], axis=0), 1)
        right = along_z(jnp.concatenate([part[5], part[1]], axis=0), -1)
        across = opposite(part[4]).astype(F32)
        up = part[2].astype(F32) + left[:pair].astype(F32) + right[pair:].astype(F32)
        down = part[6].astype(F32) + left[pair:].astype(F32) + right[:pair].astype(F32)
        up = up + jnp.where(core == 0, across, 0.0)
        down = down + jnp.where(core == 0, 0.0, across)
        total = part[0].astype(F32)
        total = total + along_z(up.astype(BF16), 2).astype(F32)
        total = total + along_z(down.astype(BF16), -2).astype(F32)
        other = across_y(total.astype(BF16)).astype(F32)
        return total + jnp.concatenate([other[rows:], other[:rows]], axis=0)

    def forward(x, weights):
        gate = contract_cols(x, weights[0]) * scale_model
        up = contract_cols(x, weights[1]) * scale_model
        hidden = (gelu_tanh(gate) * up).astype(BF16)
        return gate, up, hidden

    def backward(x, residual, down_half, gate, up, hidden):
        activated, gelu_back = jax.vjp(gelu_tanh, gate)
        grad_down = contract_rows(hidden, residual) * scale_hidden
        hidden_grad = contract_cols(residual, down_half) * scale_hidden
        gate_grad = gelu_back(hidden_grad * up)[0].astype(BF16)
        up_grad = (hidden_grad * activated).astype(BF16)
        grad_gate = contract_rows(gate_grad, x) * scale_model
        grad_up = contract_rows(up_grad, x) * scale_model
        return grad_gate, grad_up, grad_down

    def residual_of(hidden, down_half, target):
        partial = jnp.dot(hidden, down_half, preferred_element_type=F32).astype(BF16)
        output = reduce_z(partial) * scale_hidden
        return (output - target.astype(F32)).astype(BF16)

    first = jnp.concatenate([tokens[0], across_y(tokens[0])], axis=0)
    x0 = gather_z(first)
    rest = jnp.concatenate([tokens[1], targets[0], targets[1]], axis=0)
    other = across_y(rest)
    second, target0, target1 = (
        jnp.concatenate([rest[i * rows : (i + 1) * rows], other[i * rows : (i + 1) * rows]], axis=0)
        for i in range(3)
    )

    weights = (w_gate[0], w_up[0], w_down[0])
    near = tuple(with_replica(w, 1) for w in weights)

    halves = tuple(w.astype(BF16) for w in weights)
    gate, up, hidden = forward(x0, halves)
    residual = gather_z(residual_of(hidden, halves[2], target0))
    grads = tuple(g.astype(BF16) for g in backward(x0, residual, halves[2], gate, up, hidden))
    near_grads = tuple(with_replica(g, 1) for g in grads)
    weights = tuple(
        (mine + theirs) * 0.5 - (LEARNING_RATE * 0.5) * (g.astype(F32) + n.astype(F32))
        for mine, theirs, g, n in zip(weights, near, grads, near_grads)
    )
    halves = tuple(w.astype(BF16) for w in weights)

    x1 = gather_z(second)
    x1_far = with_replica(x1, 2)
    units = w_gate.shape[1]
    cut = units // 2
    mine = jnp.stack([jnp.where(core == 0, w[:cut], w[cut:]) for w in halves])
    theirs = with_replica(mine, 2)
    beside = with_replica(theirs, 1)
    low = jnp.where(core == 0, theirs, beside)
    high = jnp.where(core == 0, beside, theirs)
    far = tuple(jnp.concatenate([low[i], high[i]], axis=0) for i in range(3))

    gate, up, hidden = forward(x1, halves)
    residual = residual_of(hidden, halves[2], target1)
    residual_far = gather_z(with_replica(residual, 2))
    residual = gather_z(residual)
    grads = backward(x1, residual, halves[2], gate, up, hidden)
    gate, up, hidden = forward(x1_far, far)
    far_grads = backward(x1_far, residual_far, far[2], gate, up, hidden)
    result = tuple(
        (w + f.astype(F32)) * 0.5 - (LEARNING_RATE * 0.5) * (g + h)
        for w, f, g, h in zip(weights, far, grads, far_grads)
    )
    return tuple(w[None] for w in result)


def solution(mesh):
    n_rep, n_hid = mesh.shape["rep"], mesh.shape["hid"]
    hid_spec = P("rep", "hid", None)
    token_spec = P(None, ("rep", "hid"), None)

    def whole(tokens, targets, w_gate, w_up, w_down):
        def body(*args):
            return local(*args, n_rep=n_rep, n_z=n_hid // 2, hidden_units=w_gate.shape[1])

        return jax.shard_map(
            body,
            mesh=mesh,
            in_specs=(token_spec, token_spec, hid_spec, hid_spec, hid_spec),
            out_specs=(hid_spec, hid_spec, hid_spec),
            check_vma=False,
        )(tokens, targets, w_gate, w_up, w_down)

    return whole
```

```python
import jax
import jax.numpy as jnp
from jax import lax
from jax.sharding import PartitionSpec as P

LEARNING_RATE = 0.5
BF16, F32 = jnp.bfloat16, jnp.float32


def gelu_tanh(value):
    return jax.nn.gelu(value, approximate=True)


def contract_cols(left, right):
    return lax.dot_general(left, right, (((1,), (1,)), ((), ())), preferred_element_type=F32)


def contract_rows(left, right):
    return lax.dot_general(left, right, (((0,), (0,)), ((), ())), preferred_element_type=F32)


def local(tokens, targets, w_gate, w_up, w_down, *, n_rep, n_z, hidden_units):
    n_hid = 2 * n_z
    rows, width = tokens.shape[1], tokens.shape[2]
    pair = 2 * rows
    scale_model = float(width) ** (-0.5)
    scale_hidden = float(hidden_units) ** (-0.5)

    def along_z(value, shift):
        pairs = [(h, (h // n_z) * n_z + (h % n_z + shift) % n_z) for h in range(n_hid)]
        return lax.ppermute(value, "hid", pairs)

    def across_y(value):
        return lax.ppermute(value, "hid", [(h, h ^ n_z) for h in range(n_hid)])

    def with_replica(value, mask):
        return lax.ppermute(value, "rep", [(r, r ^ mask) for r in range(n_rep)])

    def two_along(value, sign):
        pairs = []
        for r in range(n_rep):
            step = sign * (n_z // 4) if r % 2 == 0 else -sign * (n_z // 4)
            for h in range(n_hid):
                to = (h // n_z) * n_z + (h % n_z + step) % n_z
                pairs.append((r * n_hid + h, r * n_hid + to))
        return lax.ppermute(value, ("rep", "hid"), pairs)

    def gather_far(block):
        return two_along(block, 1), two_along(block, -1)

    def gather_near(block, ahead, behind):
        across = two_along(ahead, 1)
        both = jnp.concatenate([ahead, behind], axis=0)
        left, right = along_z(both, 1), along_z(both, -1)
        return [block, ahead, behind, across, left, right]

    def gather_z(block):
        return jnp.concatenate(gather_near(block, *gather_far(block)), axis=0)

    def reduce_z(partial):
        own, ahead, behind, across = (
            partial[k * pair : (k + 1) * pair].astype(F32) for k in range(4)
        )
        across = two_along(partial[3 * pair : 4 * pair], -1)
        left = along_z(partial[4 * pair : 6 * pair], -1)
        right = along_z(partial[6 * pair :], 1)
        ahead = ahead + left[:pair].astype(F32) + right[:pair].astype(F32) + across.astype(F32)
        behind = behind + left[pair:].astype(F32) + right[pair:].astype(F32)
        ahead, behind = two_along(ahead.astype(BF16), -1), two_along(behind.astype(BF16), 1)
        total = own + ahead.astype(F32) + behind.astype(F32)
        other = across_y(total.astype(BF16)).astype(F32)
        return total + jnp.concatenate([other[rows:], other[:rows]], axis=0)

    def forward(x, weights):
        gate = contract_cols(x, weights[0]) * scale_model
        up = contract_cols(x, weights[1]) * scale_model
        hidden = (gelu_tanh(gate) * up).astype(BF16)
        return gate, up, hidden

    def backward(x, residual, down_half, gate, up, hidden):
        activated, gelu_back = jax.vjp(gelu_tanh, gate)
        grad_down = contract_rows(hidden, residual) * scale_hidden
        hidden_grad = contract_cols(residual, down_half) * scale_hidden
        gate_grad = gelu_back(hidden_grad * up)[0].astype(BF16)
        up_grad = (hidden_grad * activated).astype(BF16)
        grad_gate = contract_rows(gate_grad, x) * scale_model
        grad_up = contract_rows(up_grad, x) * scale_model
        return grad_gate, grad_up, grad_down

    def residual_of(hidden, down_half, target):
        partial = jnp.dot(hidden, down_half, preferred_element_type=F32).astype(BF16)
        output = reduce_z(partial) * scale_hidden
        return (output - target.astype(F32)).astype(BF16)

    first = jnp.concatenate([tokens[0], across_y(tokens[0])], axis=0)
    second = gather_far(tokens[1])
    x0 = gather_z(first)
    second = gather_near(tokens[1], *second)
    rest = jnp.concatenate([targets[0], targets[1]], axis=0)
    other = across_y(rest)
    target0, target1 = (
        jnp.concatenate([rest[i * rows : (i + 1) * rows], other[i * rows : (i + 1) * rows]], axis=0)
        for i in range(2)
    )

    weights = (w_gate[0], w_up[0], w_down[0])
    near = tuple(with_replica(w, 1) for w in weights)

    halves = tuple(w.astype(BF16) for w in weights)
    gate, up, hidden = forward(x0, halves)

    column = jnp.concatenate(second, axis=0)
    beside = across_y(column)
    x1 = jnp.stack(
        [column.reshape(n_z, rows, width), beside.reshape(n_z, rows, width)], axis=1
    ).reshape(n_z * pair, width)

    residual = gather_z(residual_of(hidden, halves[2], target0))
    x1_far = with_replica(x1, 2)
    grads = tuple(g.astype(BF16) for g in backward(x0, residual, halves[2], gate, up, hidden))
    near_grads = tuple(with_replica(g, 1) for g in grads)
    weights = tuple(
        (mine + theirs) * 0.5 - (LEARNING_RATE * 0.5) * (g.astype(F32) + n.astype(F32))
        for mine, theirs, g, n in zip(weights, near, grads, near_grads)
    )
    halves = tuple(w.astype(BF16) for w in weights)

    core = lax.axis_index("rep") % 2
    units = w_gate.shape[1]
    cut = units // 2

    def from_far(values):
        mine = jnp.stack([jnp.where(core == 0, w[:cut], w[cut:]) for w in values])
        theirs = with_replica(mine, 2)
        beside = with_replica(theirs, 1)
        low = jnp.where(core == 0, theirs, beside)
        high = jnp.where(core == 0, beside, theirs)
        return tuple(jnp.concatenate([low[i], high[i]], axis=0) for i in range(len(values)))

    far = from_far(halves[:2]) + from_far(halves[2:])

    gate, up, hidden = forward(x1, halves)
    residual = residual_of(hidden, halves[2], target1)
    residual_far = with_replica(residual, 2)
    residual = gather_z(residual)
    residual_far = gather_z(residual_far)
    grads = backward(x1, residual, halves[2], gate, up, hidden)
    gate, up, hidden = forward(x1_far, far)
    far_grads = backward(x1_far, residual_far, far[2], gate, up, hidden)
    result = tuple(
        (w + f.astype(F32)) * 0.5 - (LEARNING_RATE * 0.5) * (g + h)
        for w, f, g, h in zip(weights, far, grads, far_grads)
    )
    return tuple(w[None] for w in result)


def solution(mesh):
    n_rep, n_hid = mesh.shape["rep"], mesh.shape["hid"]
    hid_spec = P("rep", "hid", None)
    token_spec = P(None, ("rep", "hid"), None)

    def whole(tokens, targets, w_gate, w_up, w_down):
        def body(*args):
            return local(*args, n_rep=n_rep, n_z=n_hid // 2, hidden_units=w_gate.shape[1])

        return jax.shard_map(
            body,
            mesh=mesh,
            in_specs=(token_spec, token_spec, hid_spec, hid_spec, hid_spec),
            out_specs=(hid_spec, hid_spec, hid_spec),
            check_vma=False,
        )(tokens, targets, w_gate, w_up, w_down)

    return whole
```

```python
import functools

import jax
import jax.numpy as jnp
from jax import lax
from jax.experimental import pallas as pl
from jax.experimental.pallas import tpu as pltpu
from jax.sharding import PartitionSpec as P

LEARNING_RATE = 0.5
SQRT_2_PI = 0.7978845608028654
CUBIC = 0.044715
BF16, F32 = jnp.bfloat16, jnp.float32


def dot_nt(left, right):
    return lax.dot_general(left, right, (((1,), (1,)), ((), ())), preferred_element_type=F32)


def dot_tn(left, right):
    return lax.dot_general(left, right, (((0,), (0,)), ((), ())), preferred_element_type=F32)


def dot_nn(left, right):
    return lax.dot_general(left, right, (((1,), (0,)), ((), ())), preferred_element_type=F32)


def gelu_and_slope(value):
    inner = SQRT_2_PI * (value + CUBIC * value * value * value)
    tanh = jnp.tanh(inner)
    half = 0.5 * (1.0 + tanh)
    slope = half + 0.5 * value * (1.0 - tanh * tanh) * SQRT_2_PI * (1.0 + 3.0 * CUBIC * value * value)
    return value * half, slope


VMEM_SPEC = pl.BlockSpec(memory_space=pltpu.VMEM)


def kernel_call(body, out_shape, args, flops, scratch=(), out_specs=None):
    size = sum(v.size * v.dtype.itemsize for v in args)
    size += sum(v.size * v.dtype.itemsize for v in out_shape)
    return pl.pallas_call(
        body,
        out_shape=out_shape,
        in_specs=[VMEM_SPEC] * len(args),
        out_specs=[VMEM_SPEC] * len(out_shape) if out_specs is None else out_specs,
        scratch_shapes=list(scratch),
        cost_estimate=pl.CostEstimate(flops=flops, bytes_accessed=size, transcendentals=0),
    )(*args)


def pieces(k, pair, paired, total):
    if paired:
        return ((k * pair, 0, pair),)
    half = pair // 2
    return ((k * half, 0, half), (total // 2 + k * half, half, half))


def spread(refs, target, pair, paired):
    total = target.shape[0]
    k = 0
    for ref in refs:
        for i in range(ref.shape[0] // pair):
            for start, offset, size in pieces(k, pair, paired, total):
                target[start : start + size, :] = ref[i * pair + offset : i * pair + offset + size, :]
            k += 1


def forward_into(x, weights, saved, scale_model):
    act_ref, slope_ref, hidden_ref = saved
    gate = dot_nt(weights[0], x) * scale_model
    up = dot_nt(weights[1], x) * scale_model
    act, slope = gelu_and_slope(gate)
    act_ref[...] = act
    slope_ref[...] = slope * up
    hidden_ref[...] = (act * up).astype(BF16)


def partial_into(hidden, down, refs, pair, paired):
    total = hidden.shape[1]
    step = 384
    for c in range(0, down.shape[1], step):
        part = dot_tn(hidden, down[:, c : c + step]).astype(BF16)
        k = 0
        for ref in refs:
            for i in range(ref.shape[0] // pair):
                for start, offset, size in pieces(k, pair, paired, total):
                    ref[i * pair + offset : i * pair + offset + size, c : c + step] = part[
                        start : start + size
                    ]
                k += 1


def cast_body(gate, up, down, stacked, halves):
    for i, ref in enumerate((gate, up, down)):
        stacked[i] = ref[...]
        halves[i] = ref[...].astype(BF16)


def first_forward_body(pair, scale_model, *refs):
    blocks, targets, halves = refs[:6], refs[6], refs[7]
    x, column, act, slope, hidden = refs[8:13]
    partials = refs[13:]
    rows = pair // 2
    size = pair + rows
    k = 0
    for ref in blocks:
        for i in range(ref.shape[0] // size):
            x[k * pair : (k + 1) * pair, :] = ref[i * size : i * size + pair, :]
            column[k * rows : (k + 1) * rows, :] = ref[i * size + pair : (i + 1) * size, :]
            k += 1
    column[k * rows : (k + 1) * rows, :] = targets[0]
    column[(k + 1) * rows :, :] = targets[1]
    forward_into(x[...], (halves[0], halves[1]), (act, slope, hidden), scale_model)
    partial_into(hidden[...], halves[2], partials, pair, True)


def gradients(residual, x, act, slope, hidden, down, scales, store):
    scale_model, scale_hidden = scales
    width = x.shape[1]
    step = 384
    hidden_grad = dot_nt(down, residual[...]) * scale_hidden
    gate_grad = (hidden_grad * slope[...]).astype(BF16)
    up_grad = (hidden_grad * act[...]).astype(BF16)
    for i, left, right, scale in (
        (2, hidden[...], residual, scale_hidden),
        (0, gate_grad, x, scale_model),
        (1, up_grad, x, scale_model),
    ):
        for c in range(0, width, step):
            store(i, slice(c, c + step), dot_nn(left, right[:, c : c + step]) * scale)


def first_backward_body(pair, scales, *refs):
    blocks = refs[:6]
    x, act, slope, hidden, halves, grads, residual = refs[6:]
    spread(blocks, residual, pair, True)

    def store(i, columns, value):
        grads[i, :, columns] = value.astype(BF16)

    gradients(residual, x, act, slope, hidden, halves[2], scales, store)


def update_forward_body(pair, scale_model, *refs):
    mine, near, grads, near_grads, x, weights, halves, act, slope, hidden = refs[:10]
    partials = refs[10:]
    for i in range(3):
        moved = grads[i].astype(F32) + near_grads[i].astype(F32)
        value = (mine[i] + near[i]) * 0.5 - (LEARNING_RATE * 0.5) * moved
        weights[i] = value
        halves[i] = value.astype(BF16)
    forward_into(x[...], (halves[0], halves[1]), (act, slope, hidden), scale_model)
    partial_into(hidden[...], halves[2], partials, pair, False)


def far_forward_body(scale_model, core, x, direct, beside, weights, act, slope, hidden):
    size = direct.shape[1]
    last = weights.shape[1] - size

    @pl.when(core[0] == 0)
    def _():
        weights[:, :size, :] = direct[...]
        weights[:, last:, :] = beside[...]

    @pl.when(core[0] != 0)
    def _():
        weights[:, :size, :] = beside[...]
        weights[:, last:, :] = direct[...]

    forward_into(x[...], (weights[0], weights[1]), (act, slope, hidden), scale_model)


def own_backward_body(pair, scales, *refs):
    blocks = refs[:6]
    x, act, slope, hidden, halves, weights, total, residual = refs[6:]
    spread(blocks, residual, pair, False)

    def store(i, columns, value):
        total[i, :, columns] = weights[i, :, columns] * 0.5 - (LEARNING_RATE * 0.5) * value

    gradients(residual, x, act, slope, hidden, halves[2], scales, store)


def last_body(pair, scales, *refs):
    blocks = refs[:6]
    x, act, slope, hidden, far, total, out_gate, out_up, out_down, residual, staged, sems = refs[6:]
    outs = (out_gate, out_up, out_down)
    spread(blocks, residual, pair, False)
    copies = []

    def store(i, columns, value):
        mean = total[i, :, columns] + far[i, :, columns].astype(F32) * 0.5
        staged[i, :, columns] = mean - (LEARNING_RATE * 0.5) * value
        copy = pltpu.make_async_copy(
            staged.at[i, :, columns], outs[i].at[0, :, columns], sems.at[len(copies)]
        )
        copy.start()
        copies.append(copy)

    gradients(residual, x, act, slope, hidden, far[2], scales, store)
    for copy in copies:
        copy.wait()


def local(tokens, targets, w_gate, w_up, w_down, *, n_rep, n_z, hidden_units):
    n_hid = 2 * n_z
    rows, width = tokens.shape[1], tokens.shape[2]
    pair = 2 * rows
    scale_model = float(width) ** (-0.5)
    scale_hidden = float(hidden_units) ** (-0.5)

    def along_z(value, shift):
        pairs = [(h, (h // n_z) * n_z + (h % n_z + shift) % n_z) for h in range(n_hid)]
        return lax.ppermute(value, "hid", pairs)

    def across_y(value):
        return lax.ppermute(value, "hid", [(h, h ^ n_z) for h in range(n_hid)])

    def with_replica(value, mask):
        return lax.ppermute(value, "rep", [(r, r ^ mask) for r in range(n_rep)])

    def two_along(value, sign):
        pairs = []
        for r in range(n_rep):
            step = sign * (n_z // 4) if r % 2 == 0 else -sign * (n_z // 4)
            for h in range(n_hid):
                to = (h // n_z) * n_z + (h % n_z + step) % n_z
                pairs.append((r * n_hid + h, r * n_hid + to))
        return lax.ppermute(value, ("rep", "hid"), pairs)

    def gather_far(block):
        return two_along(block, 1), two_along(block, -1)

    def gather_near(block, ahead, behind):
        across = two_along(ahead, 1)
        both = jnp.concatenate([ahead, behind], axis=0)
        left, right = along_z(both, 1), along_z(both, -1)
        return [block, ahead, behind, across, left, right]

    def gather_z(block):
        return gather_near(block, *gather_far(block))

    def reduce_z(partials):
        own, ahead, behind, across, left, right = partials
        own, ahead, behind = (v.astype(F32) for v in (own, ahead, behind))
        across = two_along(across, -1)
        left, right = along_z(left, -1), along_z(right, 1)
        ahead = ahead + left[:pair].astype(F32) + right[:pair].astype(F32) + across.astype(F32)
        behind = behind + left[pair:].astype(F32) + right[pair:].astype(F32)
        ahead, behind = two_along(ahead.astype(BF16), -1), two_along(behind.astype(BF16), 1)
        total = own + ahead.astype(F32) + behind.astype(F32)
        other = across_y(total.astype(BF16)).astype(F32)
        return total + jnp.concatenate([other[rows:], other[:rows]], axis=0)

    def residual_of(partials, target):
        output = reduce_z(partials) * scale_hidden
        return (output - target.astype(F32)).astype(BF16)

    units = w_gate.shape[1]
    count = n_z * pair
    product = 2 * units * count * width
    scales = (scale_model, scale_hidden)

    def arr(shape, dtype):
        return jax.ShapeDtypeStruct(shape, dtype)

    stack_f32, stack_bf16 = arr((3, units, width), F32), arr((3, units, width), BF16)
    acts = [arr((units, count), F32), arr((units, count), F32), arr((units, count), BF16)]
    travel = [arr((pair, width), BF16)] * 4 + [arr((2 * pair, width), BF16)] * 2
    tokens_shape = arr((count, width), BF16)
    residual_scratch = (pltpu.VMEM((count, width), BF16),)

    first = jnp.concatenate([tokens[0], across_y(tokens[0]), tokens[1]], axis=0)
    mine, halves = kernel_call(
        cast_body, [stack_f32, stack_bf16], (w_gate[0], w_up[0], w_down[0]), 0
    )
    near = with_replica(mine, 1)
    blocks = gather_z(first)

    x0, column, act, slope, hidden, *partials = kernel_call(
        functools.partial(first_forward_body, pair, scale_model),
        [tokens_shape, arr((n_z * rows + pair, width), BF16), *acts, *travel],
        (*blocks, targets, halves),
        3 * product,
    )
    beside = across_y(column)
    half = n_z * rows
    x1 = jnp.concatenate([column[:half], beside[:half]], axis=0)
    target0, target1 = (
        jnp.concatenate([targets[i], beside[half + i * rows : half + (i + 1) * rows]], axis=0)
        for i in range(2)
    )

    blocks = gather_z(residual_of(partials, target0))
    x1_far = with_replica(x1, 2)
    (grads,) = kernel_call(
        functools.partial(first_backward_body, pair, scales),
        [stack_bf16],
        (*blocks, x0, act, slope, hidden, halves),
        4 * product,
        residual_scratch,
    )
    near_grads = with_replica(grads, 1)
    weights, halves, act, slope, hidden, *partials = kernel_call(
        functools.partial(update_forward_body, pair, scale_model),
        [stack_f32, stack_bf16, *acts, *travel],
        (mine, near, grads, near_grads, x1),
        3 * product,
    )

    core = lax.axis_index("rep") % 2
    cut = -(-units // 32) * 16
    sent = lax.dynamic_slice(halves, (0, core * (units - cut), 0), (3, cut, width))
    direct_in = with_replica(sent[:1], 2)
    direct_out = with_replica(sent[1:], 2)
    direct = jnp.concatenate([direct_in, direct_out], axis=0)
    passed = with_replica(direct, 1)

    residual = residual_of(partials, target1)
    residual_far = with_replica(residual, 2)
    blocks = gather_z(residual)
    far_blocks = gather_z(residual_far)
    (total,) = kernel_call(
        functools.partial(own_backward_body, pair, scales),
        [stack_f32],
        (*blocks, x1, act, slope, hidden, halves, weights),
        4 * product,
        residual_scratch,
    )
    far, act, slope, hidden = pl.pallas_call(
        functools.partial(far_forward_body, scale_model),
        name="k_far_forward",
        out_shape=[stack_bf16, *acts],
        in_specs=[pl.BlockSpec(memory_space=pltpu.SMEM)] + [VMEM_SPEC] * 3,
        out_specs=[VMEM_SPEC] * 4,
        cost_estimate=pl.CostEstimate(flops=2 * product, bytes_accessed=10000000, transcendentals=0),
    )(core.astype(jnp.int32).reshape(1), x1_far, direct, passed)
    return kernel_call(
        functools.partial(last_body, pair, scales),
        [arr((1, units, width), F32)] * 3,
        (*far_blocks, x1_far, act, slope, hidden, far, total),
        4 * product,
        (
            *residual_scratch,
            pltpu.VMEM((3, units, width), F32),
            pltpu.SemaphoreType.DMA((3 * (width // 384),)),
        ),
        [pl.BlockSpec(memory_space=pl.ANY)] * 3,
    )


def solution(mesh):
    n_rep, n_hid = mesh.shape["rep"], mesh.shape["hid"]
    hid_spec = P("rep", "hid", None)
    token_spec = P(None, ("rep", "hid"), None)

    def whole(tokens, targets, w_gate, w_up, w_down):
        def body(*args):
            return local(*args, n_rep=n_rep, n_z=n_hid // 2, hidden_units=w_gate.shape[1])

        return jax.shard_map(
            body,
            mesh=mesh,
            in_specs=(token_spec, token_spec, hid_spec, hid_spec, hid_spec),
            out_specs=(hid_spec, hid_spec, hid_spec),
            check_vma=False,
        )(tokens, targets, w_gate, w_up, w_down)

    return whole
```

```python
import functools

import jax
import jax.numpy as jnp
from jax import lax
from jax.experimental import pallas as pl
from jax.experimental.pallas import tpu as pltpu
from jax.sharding import PartitionSpec as P

LEARNING_RATE = 0.5
SQRT_2_PI = 0.7978845608028654
CUBIC = 0.044715
LIMIT = 12
BF16, F32 = jnp.bfloat16, jnp.float32


def dot_nt(left, right):
    return lax.dot_general(left, right, (((1,), (1,)), ((), ())), preferred_element_type=F32)


def dot_tn(left, right):
    return lax.dot_general(left, right, (((0,), (0,)), ((), ())), preferred_element_type=F32)


def dot_nn(left, right):
    return lax.dot_general(left, right, (((1,), (0,)), ((), ())), preferred_element_type=F32)


def gelu_and_slope(value):
    inner = SQRT_2_PI * (value + CUBIC * value * value * value)
    tanh = jnp.tanh(inner)
    half = 0.5 * (1.0 + tanh)
    slope = half + 0.5 * value * (1.0 - tanh * tanh) * SQRT_2_PI * (1.0 + 3.0 * CUBIC * value * value)
    return value * half, slope


VMEM_SPEC = pl.BlockSpec(memory_space=pltpu.VMEM)


def kernel_call(body, out_shape, args, flops, limit, scratch=(), out_specs=None, alias=None):
    size = sum(v.size * v.dtype.itemsize for v in args)
    size += sum(v.size * v.dtype.itemsize for v in out_shape)
    return pl.pallas_call(
        body,
        out_shape=out_shape,
        in_specs=[VMEM_SPEC] * len(args),
        out_specs=[VMEM_SPEC] * len(out_shape) if out_specs is None else out_specs,
        scratch_shapes=list(scratch),
        cost_estimate=pl.CostEstimate(flops=flops, bytes_accessed=size, transcendentals=0),
        compiler_params=pltpu.CompilerParams(vmem_limit_bytes=limit * 2**20),
        input_output_aliases=alias or {},
    )(*args)


def pieces(k, pair, paired, total):
    if paired:
        return ((k * pair, 0, pair),)
    half = pair // 2
    return ((k * half, 0, half), (total // 2 + k * half, half, half))


def spread(refs, target, pair, paired):
    total = target.shape[0]
    k = 0
    for ref in refs:
        for i in range(ref.shape[0] // pair):
            for start, offset, size in pieces(k, pair, paired, total):
                target[start : start + size, :] = ref[i * pair + offset : i * pair + offset + size, :]
            k += 1


def column_chunks(width):
    cut = width // 2 // 256 * 256
    return ((0, cut), (cut, width))


def forward_into(x, weights, saved, scale_model):
    act_ref, slope_ref, hidden_ref = saved
    gate = dot_nt(weights[0], x) * scale_model
    up = dot_nt(weights[1], x) * scale_model
    act, slope = gelu_and_slope(gate)
    act_ref[...] = act
    slope_ref[...] = slope * up
    hidden_ref[...] = (act * up).astype(BF16)


def partial_into(hidden, down, refs, pair, paired):
    total = hidden.shape[1]
    for c, end in column_chunks(down.shape[1]):
        part = dot_tn(hidden, down[:, c:end]).astype(BF16)
        k = 0
        for ref in refs:
            for i in range(ref.shape[0] // pair):
                for start, offset, size in pieces(k, pair, paired, total):
                    ref[i * pair + offset : i * pair + offset + size, c:end] = part[
                        start : start + size
                    ]
                k += 1


def cast_body(gate, up, down, stacked, halves):
    for i, ref in enumerate((gate, up, down)):
        stacked[i] = ref[...]
        halves[i] = ref[...].astype(BF16)


def first_forward_body(pair, scale_model, *refs):
    blocks, targets, halves = refs[:6], refs[6], refs[7]
    x, column, act, slope, hidden = refs[8:13]
    partials = refs[13:]
    rows = pair // 2
    size = pair + rows
    k = 0
    for ref in blocks:
        for i in range(ref.shape[0] // size):
            x[k * pair : (k + 1) * pair, :] = ref[i * size : i * size + pair, :]
            column[k * rows : (k + 1) * rows, :] = ref[i * size + pair : (i + 1) * size, :]
            k += 1
    column[k * rows : (k + 1) * rows, :] = targets[0]
    column[(k + 1) * rows :, :] = targets[1]
    forward_into(x[...], (halves[0], halves[1]), (act, slope, hidden), scale_model)
    partial_into(hidden[...], halves[2], partials, pair, True)


def gradients(residual, x, act, slope, hidden, down, scales, store):
    scale_model, scale_hidden = scales
    width = x.shape[1]
    hidden_grad = dot_nt(down, residual[...]) * scale_hidden
    gate_grad = (hidden_grad * slope[...]).astype(BF16)
    up_grad = (hidden_grad * act[...]).astype(BF16)
    for i, left, right, scale in (
        (2, hidden[...], residual, scale_hidden),
        (0, gate_grad, x, scale_model),
        (1, up_grad, x, scale_model),
    ):
        for c, end in column_chunks(width):
            store(i, slice(c, end), dot_nn(left, right[:, c:end]) * scale)


def first_backward_body(pair, scales, *refs):
    blocks = refs[:6]
    x, act, slope, hidden, halves, grads, residual = refs[6:]
    spread(blocks, residual, pair, True)

    def store(i, columns, value):
        grads[i, :, columns] = value.astype(BF16)

    gradients(residual, x, act, slope, hidden, halves[2], scales, store)


def update_forward_body(pair, scale_model, *refs):
    mine, near, grads, near_grads, x, weights, halves, act, slope, hidden = refs[:10]
    partials = refs[10:]
    for i in range(3):
        moved = grads[i].astype(F32) + near_grads[i].astype(F32)
        value = (mine[i] + near[i]) * 0.5 - (LEARNING_RATE * 0.5) * moved
        weights[i] = value
        halves[i] = value.astype(BF16)
    forward_into(x[...], (halves[0], halves[1]), (act, slope, hidden), scale_model)
    partial_into(hidden[...], halves[2], partials, pair, False)


def far_forward_body(scale_model, core, x, direct, beside, weights, act, slope, hidden):
    size = direct.shape[1]
    last = weights.shape[1] - size

    @pl.when(core[0] == 0)
    def _():
        weights[:, :size, :] = direct[...]
        weights[:, last:, :] = beside[...]

    @pl.when(core[0] != 0)
    def _():
        weights[:, :size, :] = beside[...]
        weights[:, last:, :] = direct[...]

    forward_into(x[...], (weights[0], weights[1]), (act, slope, hidden), scale_model)


def own_backward_body(pair, scales, *refs):
    blocks = refs[:6]
    x, act, slope, hidden, halves, weights, total, residual = refs[6:]
    spread(blocks, residual, pair, False)

    def store(i, columns, value):
        total[i, :, columns] = weights[i, :, columns] * 0.5 - (LEARNING_RATE * 0.5) * value

    gradients(residual, x, act, slope, hidden, halves[2], scales, store)


def last_body(pair, scales, *refs):
    blocks = refs[:6]
    x, act, slope, hidden, far, total, out_gate, out_up, out_down, residual, staged, sems = refs[6:]
    outs = (out_gate, out_up, out_down)
    spread(blocks, residual, pair, False)
    copies = []

    def store(i, columns, value):
        mean = total[i, :, columns] + far[i, :, columns].astype(F32) * 0.5
        staged[i, :, columns] = mean - (LEARNING_RATE * 0.5) * value
        copy = pltpu.make_async_copy(
            staged.at[i, :, columns], outs[i].at[0, :, columns], sems.at[len(copies)]
        )
        copy.start()
        copies.append(copy)

    gradients(residual, x, act, slope, hidden, far[2], scales, store)
    for copy in copies:
        copy.wait()


def local(tokens, targets, w_gate, w_up, w_down, *, n_rep, n_z, hidden_units):
    n_hid = 2 * n_z
    rows, width = tokens.shape[1], tokens.shape[2]
    pair = 2 * rows
    scale_model = float(width) ** (-0.5)
    scale_hidden = float(hidden_units) ** (-0.5)

    def along_z(value, shift):
        pairs = [(h, (h // n_z) * n_z + (h % n_z + shift) % n_z) for h in range(n_hid)]
        return lax.ppermute(value, "hid", pairs)

    def across_y(value):
        return lax.ppermute(value, "hid", [(h, h ^ n_z) for h in range(n_hid)])

    def with_replica(value, mask):
        return lax.ppermute(value, "rep", [(r, r ^ mask) for r in range(n_rep)])

    def two_along(value, sign):
        pairs = []
        for r in range(n_rep):
            step = sign * (n_z // 4) if r % 2 == 0 else -sign * (n_z // 4)
            for h in range(n_hid):
                to = (h // n_z) * n_z + (h % n_z + step) % n_z
                pairs.append((r * n_hid + h, r * n_hid + to))
        return lax.ppermute(value, ("rep", "hid"), pairs)

    def gather_far(block):
        return two_along(block, 1), two_along(block, -1)

    def gather_near(block, ahead, behind):
        across = two_along(ahead, 1)
        both = jnp.concatenate([ahead, behind], axis=0)
        left, right = along_z(both, 1), along_z(both, -1)
        return [block, ahead, behind, across, left, right]

    def gather_z(block):
        return gather_near(block, *gather_far(block))

    def reduce_z(partials):
        own, ahead, behind, across, left, right = partials
        own, ahead, behind = (v.astype(F32) for v in (own, ahead, behind))
        across = two_along(across, -1)
        left, right = along_z(left, -1), along_z(right, 1)
        ahead = ahead + left[:pair].astype(F32) + right[:pair].astype(F32) + across.astype(F32)
        behind = behind + left[pair:].astype(F32) + right[pair:].astype(F32)
        ahead, behind = two_along(ahead.astype(BF16), -1), two_along(behind.astype(BF16), 1)
        total = own + ahead.astype(F32) + behind.astype(F32)
        other = across_y(total.astype(BF16)).astype(F32)
        return total + jnp.concatenate([other[rows:], other[:rows]], axis=0)

    def residual_of(partials, target):
        output = reduce_z(partials) * scale_hidden
        return (output - target.astype(F32)).astype(BF16)

    units = w_gate.shape[1]
    count = n_z * pair
    product = 2 * units * count * width
    scales = (scale_model, scale_hidden)

    def arr(shape, dtype):
        return jax.ShapeDtypeStruct(shape, dtype)

    stack_f32, stack_bf16 = arr((3, units, width), F32), arr((3, units, width), BF16)
    acts = [arr((units, count), F32), arr((units, count), F32), arr((units, count), BF16)]
    travel = [arr((pair, width), BF16)] * 4 + [arr((2 * pair, width), BF16)] * 2
    tokens_shape = arr((count, width), BF16)
    residual_scratch = (pltpu.VMEM((count, width), BF16),)

    first = jnp.concatenate([tokens[0], across_y(tokens[0]), tokens[1]], axis=0)
    mine, halves = kernel_call(
        cast_body, [stack_f32, stack_bf16], (w_gate[0], w_up[0], w_down[0]), 0, LIMIT
    )
    near = with_replica(mine, 1)
    blocks = gather_z(first)

    x0, column, act, slope, hidden, *partials = kernel_call(
        functools.partial(first_forward_body, pair, scale_model),
        [tokens_shape, arr((n_z * rows + pair, width), BF16), *acts, *travel],
        (*blocks, targets, halves),
        3 * product,
        LIMIT,
    )
    beside = across_y(column)
    half = n_z * rows
    x1 = jnp.concatenate([column[:half], beside[:half]], axis=0)
    target0, target1 = (
        jnp.concatenate([targets[i], beside[half + i * rows : half + (i + 1) * rows]], axis=0)
        for i in range(2)
    )

    blocks = gather_z(residual_of(partials, target0))
    x1_far = with_replica(x1, 2)
    (grads,) = kernel_call(
        functools.partial(first_backward_body, pair, scales),
        [stack_bf16],
        (*blocks, x0, act, slope, hidden, halves),
        4 * product,
        LIMIT,
        residual_scratch,
    )
    near_grads = with_replica(grads, 1)
    weights, halves, act, slope, hidden, *partials = kernel_call(
        functools.partial(update_forward_body, pair, scale_model),
        [stack_f32, stack_bf16, *acts, *travel],
        (mine, near, grads, near_grads, x1),
        3 * product,
        LIMIT,
        alias={0: 0},
    )

    core = lax.axis_index("rep") % 2
    cut = -(-units // 32) * 16
    sent = lax.dynamic_slice(halves, (0, core * (units - cut), 0), (3, cut, width))
    direct_in = with_replica(sent[:1], 2)
    direct_out = with_replica(sent[1:], 2)
    direct = jnp.concatenate([direct_in, direct_out], axis=0)
    passed = with_replica(direct, 1)

    residual = residual_of(partials, target1)
    residual_far = with_replica(residual, 2)
    blocks = gather_z(residual)
    far_blocks = gather_z(residual_far)
    (total,) = kernel_call(
        functools.partial(own_backward_body, pair, scales),
        [stack_f32],
        (*blocks, x1, act, slope, hidden, halves, weights),
        4 * product,
        LIMIT,
        residual_scratch,
    )
    far, act, slope, hidden = pl.pallas_call(
        functools.partial(far_forward_body, scale_model),
        name="k_far_forward",
        out_shape=[stack_bf16, *acts],
        in_specs=[pl.BlockSpec(memory_space=pltpu.SMEM)] + [VMEM_SPEC] * 3,
        out_specs=[VMEM_SPEC] * 4,
        cost_estimate=pl.CostEstimate(flops=2 * product, bytes_accessed=10000000, transcendentals=0),
        compiler_params=pltpu.CompilerParams(vmem_limit_bytes=LIMIT * 2**20),
    )(core.astype(jnp.int32).reshape(1), x1_far, direct, passed)
    return kernel_call(
        functools.partial(last_body, pair, scales),
        [arr((1, units, width), F32)] * 3,
        (*far_blocks, x1_far, act, slope, hidden, far, total),
        4 * product,
        LIMIT,
        (
            *residual_scratch,
            pltpu.VMEM((3, units, width), F32),
            pltpu.SemaphoreType.DMA((6,)),
        ),
        [pl.BlockSpec(memory_space=pl.ANY)] * 3,
    )


def solution(mesh):
    n_rep, n_hid = mesh.shape["rep"], mesh.shape["hid"]
    hid_spec = P("rep", "hid", None)
    token_spec = P(None, ("rep", "hid"), None)

    def whole(tokens, targets, w_gate, w_up, w_down):
        def body(*args):
            return local(*args, n_rep=n_rep, n_z=n_hid // 2, hidden_units=w_gate.shape[1])

        return jax.shard_map(
            body,
            mesh=mesh,
            in_specs=(token_spec, token_spec, hid_spec, hid_spec, hid_spec),
            out_specs=(hid_spec, hid_spec, hid_spec),
            check_vma=False,
        )(tokens, targets, w_gate, w_up, w_down)

    return whole
```

```python
import functools

import jax
import jax.numpy as jnp
from jax import lax
from jax.experimental import pallas as pl
from jax.experimental.pallas import tpu as pltpu
from jax.sharding import PartitionSpec as P

LEARNING_RATE = 0.5
SQRT_2_PI = 0.7978845608028654
CUBIC = 0.044715
LIMIT = 12
UPDATE_LIMIT = 14
BF16, F32 = jnp.bfloat16, jnp.float32


def dot_nt(left, right):
    return lax.dot_general(left, right, (((1,), (1,)), ((), ())), preferred_element_type=F32)


def dot_nn(left, right):
    return lax.dot_general(left, right, (((1,), (0,)), ((), ())), preferred_element_type=F32)


def gelu_and_slope(value):
    inner = SQRT_2_PI * (value + CUBIC * value * value * value)
    tanh = jnp.tanh(inner)
    half = 0.5 * (1.0 + tanh)
    slope = half + 0.5 * value * (1.0 - tanh * tanh) * SQRT_2_PI * (1.0 + 3.0 * CUBIC * value * value)
    return value * half, slope


VMEM_SPEC = pl.BlockSpec(memory_space=pltpu.VMEM)
SMEM_SPEC = pl.BlockSpec(memory_space=pltpu.SMEM)
HBM_SPEC = pl.BlockSpec(memory_space=pltpu.HBM)


def kernel_call(body, out_shape, args, flops, limit, scratch=(), in_specs=None, out_specs=None, alias=None):
    size = sum(v.size * v.dtype.itemsize for v in args)
    size += sum(v.size * v.dtype.itemsize for v in out_shape)
    return pl.pallas_call(
        body,
        out_shape=out_shape,
        in_specs=[VMEM_SPEC] * len(args) if in_specs is None else in_specs,
        out_specs=[VMEM_SPEC] * len(out_shape) if out_specs is None else out_specs,
        scratch_shapes=list(scratch),
        cost_estimate=pl.CostEstimate(flops=flops, bytes_accessed=size, transcendentals=0),
        compiler_params=pltpu.CompilerParams(vmem_limit_bytes=limit * 2**20),
        input_output_aliases=alias or {},
    )(*args)


def pieces(k, pair, paired, total):
    if paired:
        return ((k * pair, 0, pair),)
    half = pair // 2
    return ((k * half, 0, half), (total // 2 + k * half, half, half))


def spread(refs, target, pair, paired):
    total = target.shape[0]
    k = 0
    for ref in refs:
        for i in range(ref.shape[0] // pair):
            for start, offset, size in pieces(k, pair, paired, total):
                target[start : start + size, :] = ref[i * pair + offset : i * pair + offset + size, :]
            k += 1


COLUMNS = 384
TOKENS = 256
UNITS = 48


def forward_into(x, weights, saved, scale_model):
    act_ref, slope_ref, hidden_ref = saved

    @pl.loop(0, x.shape[0] // TOKENS)
    def _(step):
        start = pl.multiple_of(step * TOKENS, TOKENS)
        here = pl.ds(start, TOKENS)
        batch = x[here, :]
        gate = dot_nt(weights[0], batch) * scale_model
        up = dot_nt(weights[1], batch) * scale_model
        act, slope = gelu_and_slope(gate)
        act_ref[:, here] = act
        slope_ref[:, here] = slope * up
        hidden_ref[:, here] = (act * up).astype(BF16)


def partial_into(hidden, down, refs, pair, paired, turned):
    total = hidden.shape[1]
    turned[...] = hidden[...].T

    @pl.loop(0, down.shape[1] // COLUMNS)
    def _(step):
        here = pl.ds(pl.multiple_of(step * COLUMNS, COLUMNS), COLUMNS)
        part = dot_nn(turned[...], down[:, here]).astype(BF16)
        k = 0
        for ref in refs:
            for i in range(ref.shape[0] // pair):
                for start, offset, size in pieces(k, pair, paired, total):
                    ref[i * pair + offset : i * pair + offset + size, here] = part[
                        start : start + size
                    ]
                k += 1


def cast_body(gate, up, down, stacked, halves):
    for i, ref in enumerate((gate, up, down)):
        stacked[i] = ref[...]
        halves[i] = ref[...].astype(BF16)


def mean_body(mine, near, base):
    for i in range(3):

        @pl.loop(0, mine.shape[1] // UNITS)
        def _(step):
            here = pl.ds(pl.multiple_of(step * UNITS, UNITS), UNITS)
            base[i, here, :] = (mine[i, here, :] + near[i, here, :]) * 0.5


def first_forward_body(pair, scale_model, *refs):
    blocks, targets, halves = refs[:6], refs[6], refs[7]
    x, column, act, slope, hidden = refs[8:13]
    partials, turned = refs[13:19], refs[19]
    rows = pair // 2
    size = pair + rows
    k = 0
    for ref in blocks:
        for i in range(ref.shape[0] // size):
            x[k * pair : (k + 1) * pair, :] = ref[i * size : i * size + pair, :]
            column[k * rows : (k + 1) * rows, :] = ref[i * size + pair : (i + 1) * size, :]
            k += 1
    column[k * rows : (k + 1) * rows, :] = targets[0]
    column[(k + 1) * rows :, :] = targets[1]
    forward_into(x, halves, (act, slope, hidden), scale_model)
    partial_into(hidden, halves.at[2], partials, pair, True, turned)


def gradients(residual, x, act, slope, hidden, down, scales, saved, store):
    scale_model, scale_hidden = scales
    gate_grad, up_grad = saved

    @pl.loop(0, x.shape[0] // TOKENS)
    def _(step):
        here = pl.ds(pl.multiple_of(step * TOKENS, TOKENS), TOKENS)
        hidden_grad = dot_nt(down[...], residual[here, :]) * scale_hidden
        gate_grad[:, here] = (hidden_grad * slope[:, here]).astype(BF16)
        up_grad[:, here] = (hidden_grad * act[:, here]).astype(BF16)

    @pl.loop(0, x.shape[1] // COLUMNS)
    def _(step):
        here = pl.ds(pl.multiple_of(step * COLUMNS, COLUMNS), COLUMNS)
        store(2, step, here, dot_nn(hidden[...], residual[:, here]) * scale_hidden)
        store(0, step, here, dot_nn(gate_grad[...], x[:, here]) * scale_model)
        store(1, step, here, dot_nn(up_grad[...], x[:, here]) * scale_model)


def first_backward_body(pair, scales, *refs):
    blocks = refs[:6]
    x, act, slope, hidden, halves, grads, residual, *saved = refs[6:]
    spread(blocks, residual, pair, True)

    def store(i, step, columns, value):
        grads[i, :, columns] = value.astype(BF16)

    gradients(residual, x, act, slope, hidden, halves.at[2], scales, saved, store)


def update_forward_body(pair, scale_model, *refs):
    core, base, grads, near_grads, x = refs[:5]
    kept, sent_in, sent_out = refs[5:10], refs[10], refs[11]
    partials, halves, turned = refs[12:18], refs[18], refs[19]
    size = sent_in.shape[1]
    last = halves.shape[1] - size
    weights, act, slope, hidden, down = kept

    for i in range(3):

        @pl.loop(0, base.shape[1] // UNITS)
        def _(step):
            here = pl.ds(pl.multiple_of(step * UNITS, UNITS), UNITS)
            moved = grads[i, here, :].astype(F32) + near_grads[i, here, :].astype(F32)
            value = base[i, here, :] - (LEARNING_RATE * 0.5) * moved
            weights[i, here, :] = value
            halves[i, here, :] = value.astype(BF16)

    down[...] = halves[2]
    forward_into(x, halves, (act, slope, hidden), scale_model)
    partial_into(hidden, halves.at[2], partials, pair, False, turned)

    @pl.when(core[0] == 0)
    def _():
        sent_in[0] = halves[0, :size, :]
        sent_out[...] = halves[1:, :size, :]

    @pl.when(core[0] != 0)
    def _():
        sent_in[0] = halves[0, last:, :]
        sent_out[...] = halves[1:, last:, :]


def far_forward_body(scale_model, core, x, direct_in, direct_out, beside, weights, act, slope, hidden):
    size = direct_in.shape[1]
    last = weights.shape[1] - size

    @pl.when(core[0] == 0)
    def _():
        weights[0, :size, :] = direct_in[0]
        weights[1:, :size, :] = direct_out[...]
        weights[:, last:, :] = beside[...]

    @pl.when(core[0] != 0)
    def _():
        weights[:, :size, :] = beside[...]
        weights[0, last:, :] = direct_in[0]
        weights[1:, last:, :] = direct_out[...]

    forward_into(x, weights, (act, slope, hidden), scale_model)


def join_body(direct_in, direct_out, joined):
    joined[0] = direct_in[0]
    joined[1:] = direct_out[...]


def own_backward_body(pair, scales, *refs):
    blocks = refs[:6]
    x, act, slope, hidden, down, weights, total, residual, *saved = refs[6:]
    spread(blocks, residual, pair, False)

    def store(i, step, columns, value):
        total[i, :, columns] = weights[i, :, columns] * 0.5 - (LEARNING_RATE * 0.5) * value

    gradients(residual, x, act, slope, hidden, down, scales, saved, store)


def last_body(pair, scales, *refs):
    blocks = refs[:6]
    x, act, slope, hidden, far, total, out_gate, out_up, out_down, residual, staged, sems, *saved = refs[6:]
    outs = (out_gate, out_up, out_down)
    spread(blocks, residual, pair, False)

    def out_copy(i, step, columns):
        return pltpu.make_async_copy(
            staged.at[i, :, columns], outs[i].at[0, :, columns], sems.at[i, step]
        )

    def store(i, step, columns, value):
        mean = total[i, :, columns] + far[i, :, columns].astype(F32) * 0.5
        staged[i, :, columns] = mean - (LEARNING_RATE * 0.5) * value
        out_copy(i, step, columns).start()

    gradients(residual, x, act, slope, hidden, far.at[2], scales, saved, store)
    for i in (2, 0, 1):
        for step in range(x.shape[1] // COLUMNS):
            out_copy(i, step, slice(step * COLUMNS, (step + 1) * COLUMNS)).wait()


def local(tokens, targets, w_gate, w_up, w_down, *, n_rep, n_z, hidden_units):
    n_hid = 2 * n_z
    rows, width = tokens.shape[1], tokens.shape[2]
    pair = 2 * rows
    scale_model = float(width) ** (-0.5)
    scale_hidden = float(hidden_units) ** (-0.5)

    def along_z(value, shift):
        pairs = [(h, (h // n_z) * n_z + (h % n_z + shift) % n_z) for h in range(n_hid)]
        return lax.ppermute(value, "hid", pairs)

    def across_y(value):
        return lax.ppermute(value, "hid", [(h, h ^ n_z) for h in range(n_hid)])

    def with_replica(value, mask):
        return lax.ppermute(value, "rep", [(r, r ^ mask) for r in range(n_rep)])

    def two_along(value, sign):
        pairs = []
        for r in range(n_rep):
            step = sign * (n_z // 4) if r % 2 == 0 else -sign * (n_z // 4)
            for h in range(n_hid):
                to = (h // n_z) * n_z + (h % n_z + step) % n_z
                pairs.append((r * n_hid + h, r * n_hid + to))
        return lax.ppermute(value, ("rep", "hid"), pairs)

    def gather_far(block):
        return two_along(block, 1), two_along(block, -1)

    def gather_near(block, ahead, behind):
        across = two_along(ahead, 1)
        both = jnp.concatenate([ahead, behind], axis=0)
        left, right = along_z(both, 1), along_z(both, -1)
        return [block, ahead, behind, across, left, right]

    def gather_z(block):
        return gather_near(block, *gather_far(block))

    def reduce_z(partials):
        own, ahead, behind, across, left, right = partials
        own, ahead, behind = (v.astype(F32) for v in (own, ahead, behind))
        across = two_along(across, -1)
        left, right = along_z(left, -1), along_z(right, 1)
        ahead = ahead + left[:pair].astype(F32) + right[:pair].astype(F32) + across.astype(F32)
        behind = behind + left[pair:].astype(F32) + right[pair:].astype(F32)
        ahead, behind = two_along(ahead.astype(BF16), -1), two_along(behind.astype(BF16), 1)
        total = own + ahead.astype(F32) + behind.astype(F32)
        other = across_y(total.astype(BF16)).astype(F32)
        return total + jnp.concatenate([other[rows:], other[:rows]], axis=0)

    def residual_of(partials, target):
        output = reduce_z(partials) * scale_hidden
        return (output - target.astype(F32)).astype(BF16)

    units = w_gate.shape[1]
    count = n_z * pair
    product = 2 * units * count * width
    scales = (scale_model, scale_hidden)

    def arr(shape, dtype):
        return jax.ShapeDtypeStruct(shape, dtype)

    stack_f32, stack_bf16 = arr((3, units, width), F32), arr((3, units, width), BF16)
    acts = [arr((units, count), F32), arr((units, count), F32), arr((units, count), BF16)]
    travel = [arr((pair, width), BF16)] * 4 + [arr((2 * pair, width), BF16)] * 2
    tokens_shape = arr((count, width), BF16)
    grad_scratch = (pltpu.VMEM((units, count), BF16),) * 2
    residual_scratch = pltpu.VMEM((count, width), BF16)
    turned_scratch = pltpu.VMEM((count, units), BF16)

    first = jnp.concatenate([tokens[0], across_y(tokens[0]), tokens[1]], axis=0)
    mine, halves = kernel_call(
        cast_body, [stack_f32, stack_bf16], (w_gate[0], w_up[0], w_down[0]), 0, LIMIT
    )
    near = with_replica(mine, 1)
    blocks = gather_z(first)

    x0, column, act, slope, hidden, *partials = kernel_call(
        functools.partial(first_forward_body, pair, scale_model),
        [tokens_shape, arr((n_z * rows + pair, width), BF16), *acts, *travel],
        (*blocks, targets, halves),
        3 * product,
        LIMIT,
        (turned_scratch,),
    )
    beside = across_y(column)
    half = n_z * rows
    x1 = jnp.concatenate([column[:half], beside[:half]], axis=0)
    target0, target1 = (
        jnp.concatenate([targets[i], beside[half + i * rows : half + (i + 1) * rows]], axis=0)
        for i in range(2)
    )

    blocks = gather_z(residual_of(partials, target0))
    x1_far = with_replica(x1, 2)
    (grads,) = kernel_call(
        functools.partial(first_backward_body, pair, scales),
        [stack_bf16],
        (*blocks, x0, act, slope, hidden, halves),
        4 * product,
        LIMIT,
        (residual_scratch, *grad_scratch),
    )
    near_grads = with_replica(grads, 1)

    (base,) = kernel_call(mean_body, [stack_f32], (mine, near), 0, UPDATE_LIMIT)

    core = (lax.axis_index("rep") % 2).astype(jnp.int32).reshape(1)
    cut = -(-units // 32) * 16
    weights, act, slope, hidden, down, sent_in, sent_out, *partials = kernel_call(
        functools.partial(update_forward_body, pair, scale_model),
        [
            stack_f32,
            *acts,
            arr((units, width), BF16),
            arr((1, cut, width), BF16),
            arr((2, cut, width), BF16),
            *travel,
        ],
        (core, base, grads, near_grads, x1),
        3 * product,
        UPDATE_LIMIT,
        (
            pltpu.VMEM((3, units, width), BF16),
            turned_scratch,
        ),
        [SMEM_SPEC] + [VMEM_SPEC] * 4,
    )
    direct_in = with_replica(sent_in, 2)
    direct_out = with_replica(sent_out, 2)
    (direct,) = kernel_call(join_body, [arr((3, cut, width), BF16)], (direct_in, direct_out), 0, 12)
    passed = with_replica(direct, 1)

    residual = residual_of(partials, target1)
    residual_far = with_replica(residual, 2)
    blocks = gather_z(residual)
    far_blocks = gather_z(residual_far)
    (total,) = kernel_call(
        functools.partial(own_backward_body, pair, scales),
        [stack_f32],
        (*blocks, x1, act, slope, hidden, down, weights),
        4 * product,
        LIMIT,
        (residual_scratch, *grad_scratch),
    )
    far, act, slope, hidden = kernel_call(
        functools.partial(far_forward_body, scale_model),
        [stack_bf16, *acts],
        (core, x1_far, direct_in, direct_out, passed),
        2 * product,
        LIMIT,
        (),
        [SMEM_SPEC] + [VMEM_SPEC] * 4,
    )
    return kernel_call(
        functools.partial(last_body, pair, scales),
        [arr((1, units, width), F32)] * 3,
        (*far_blocks, x1_far, act, slope, hidden, far, total),
        4 * product,
        LIMIT,
        (
            residual_scratch,
            pltpu.VMEM((3, units, width), F32),
            pltpu.SemaphoreType.DMA((3, width // COLUMNS)),
            *grad_scratch,
        ),
        None,
        [pl.BlockSpec(memory_space=pl.ANY)] * 3,
    )


def solution(mesh):
    n_rep, n_hid = mesh.shape["rep"], mesh.shape["hid"]
    hid_spec = P("rep", "hid", None)
    token_spec = P(None, ("rep", "hid"), None)

    def whole(tokens, targets, w_gate, w_up, w_down):
        def body(*args):
            return local(*args, n_rep=n_rep, n_z=n_hid // 2, hidden_units=w_gate.shape[1])

        return jax.shard_map(
            body,
            mesh=mesh,
            in_specs=(token_spec, token_spec, hid_spec, hid_spec, hid_spec),
            out_specs=(hid_spec, hid_spec, hid_spec),
            check_vma=False,
        )(tokens, targets, w_gate, w_up, w_down)

    return whole
```

```python
import functools

import jax
import jax.numpy as jnp
from jax import lax
from jax.experimental import pallas as pl
from jax.experimental.pallas import tpu as pltpu
from jax.sharding import PartitionSpec as P

LEARNING_RATE = 0.5
SQRT_2_PI = 0.7978845608028654
CUBIC = 0.044715
LIMIT = 12
UPDATE_LIMIT = 14
BF16, F32 = jnp.bfloat16, jnp.float32


def dot_nt(left, right):
    return lax.dot_general(left, right, (((1,), (1,)), ((), ())), preferred_element_type=F32)


def dot_nn(left, right):
    return lax.dot_general(left, right, (((1,), (0,)), ((), ())), preferred_element_type=F32)


def gelu_and_slope(value):
    inner = SQRT_2_PI * (value + CUBIC * value * value * value)
    tanh = jnp.tanh(inner)
    half = 0.5 * (1.0 + tanh)
    slope = half + 0.5 * value * (1.0 - tanh * tanh) * SQRT_2_PI * (1.0 + 3.0 * CUBIC * value * value)
    return value * half, slope


VMEM_SPEC = pl.BlockSpec(memory_space=pltpu.VMEM)
SMEM_SPEC = pl.BlockSpec(memory_space=pltpu.SMEM)
HBM_SPEC = pl.BlockSpec(memory_space=pltpu.HBM)


def kernel_call(body, out_shape, args, flops, limit, scratch=(), in_specs=None, out_specs=None, alias=None):
    size = sum(v.size * v.dtype.itemsize for v in args)
    size += sum(v.size * v.dtype.itemsize for v in out_shape)
    return pl.pallas_call(
        body,
        out_shape=out_shape,
        in_specs=[VMEM_SPEC] * len(args) if in_specs is None else in_specs,
        out_specs=[VMEM_SPEC] * len(out_shape) if out_specs is None else out_specs,
        scratch_shapes=list(scratch),
        cost_estimate=pl.CostEstimate(flops=flops, bytes_accessed=size, transcendentals=0),
        compiler_params=pltpu.CompilerParams(vmem_limit_bytes=limit * 2**20),
        input_output_aliases=alias or {},
    )(*args)


def pieces(k, pair, paired, total):
    if paired:
        return ((k * pair, 0, pair),)
    half = pair // 2
    return ((k * half, 0, half), (total // 2 + k * half, half, half))


def spread(refs, target, pair, paired):
    total = target.shape[0]
    k = 0
    for ref in refs:
        for i in range(ref.shape[0] // pair):
            for start, offset, size in pieces(k, pair, paired, total):
                target[start : start + size, :] = ref[i * pair + offset : i * pair + offset + size, :]
            k += 1


COLUMNS = 384
TOKENS = 256
UNITS = 48
PART = 16


def forward_into(x, weights, saved, scale_model):
    act_ref, slope_ref, hidden_ref = saved

    @pl.loop(0, x.shape[0] // TOKENS)
    def _(step):
        start = pl.multiple_of(step * TOKENS, TOKENS)
        here = pl.ds(start, TOKENS)
        batch = x[here, :]
        gate = dot_nt(weights[0], batch) * scale_model
        up = dot_nt(weights[1], batch) * scale_model
        act, slope = gelu_and_slope(gate)
        act_ref[:, here] = act
        slope_ref[:, here] = slope * up
        hidden_ref[:, here] = (act * up).astype(BF16)


def partial_into(hidden, down, refs, pair, paired, turned):
    total = hidden.shape[1]
    turned[...] = hidden[...].T

    @pl.loop(0, down.shape[1] // COLUMNS)
    def _(step):
        here = pl.ds(pl.multiple_of(step * COLUMNS, COLUMNS), COLUMNS)
        part = dot_nn(turned[...], down[:, here]).astype(BF16)
        k = 0
        for ref in refs:
            for i in range(ref.shape[0] // pair):
                for start, offset, size in pieces(k, pair, paired, total):
                    ref[i * pair + offset : i * pair + offset + size, here] = part[
                        start : start + size
                    ]
                k += 1


def each_part(total, size, body):
    @pl.loop(0, total // size)
    def _(step):
        body(pl.multiple_of(step * size, size))


def cast_body(gate, up, down, stacked, halves):
    def one(start):
        here = pl.ds(start, UNITS)
        for i, ref in enumerate((gate, up, down)):
            stacked[i, here, :] = ref[here, :]
            halves[i, here, :] = ref[here, :].astype(BF16)

    each_part(gate.shape[0], UNITS, one)


def mean_body(mine, near, base):
    for i in range(3):

        @pl.loop(0, mine.shape[1] // UNITS)
        def _(step):
            here = pl.ds(pl.multiple_of(step * UNITS, UNITS), UNITS)
            base[i, here, :] = (mine[i, here, :] + near[i, here, :]) * 0.5


def first_forward_body(pair, scale_model, *refs):
    blocks, targets, halves = refs[:6], refs[6], refs[7]
    x, column, act, slope, hidden = refs[8:13]
    partials, turned = refs[13:19], refs[19]
    rows = pair // 2
    size = pair + rows
    k = 0
    for ref in blocks:
        for i in range(ref.shape[0] // size):
            x[k * pair : (k + 1) * pair, :] = ref[i * size : i * size + pair, :]
            column[k * rows : (k + 1) * rows, :] = ref[i * size + pair : (i + 1) * size, :]
            k += 1
    column[k * rows : (k + 1) * rows, :] = targets[0]
    column[(k + 1) * rows :, :] = targets[1]
    forward_into(x, halves, (act, slope, hidden), scale_model)
    partial_into(hidden, halves.at[2], partials, pair, True, turned)


def gradients(residual, x, act, slope, hidden, down, scales, saved, store, tight):
    scale_model, scale_hidden = scales

    @pl.loop(0, x.shape[0] // TOKENS)
    def _(step):
        here = pl.ds(pl.multiple_of(step * TOKENS, TOKENS), TOKENS)
        hidden_grad = dot_nt(down[...], residual[here, :]) * scale_hidden
        saved[0, :, here] = (hidden_grad * slope[:, here]).astype(BF16)
        saved[1, :, here] = (hidden_grad * act[:, here]).astype(BF16)

    @pl.loop(0, x.shape[1] // COLUMNS)
    def _(step):
        here = pl.ds(pl.multiple_of(step * COLUMNS, COLUMNS), COLUMNS)
        store(2, step, here, dot_nn(hidden[...], residual[:, here]) * scale_hidden)

        def one(i):
            store(i, step, here, dot_nn(saved[i], x[:, here]) * scale_model)

        if tight:
            pl.loop(0, 2)(one)
        else:
            one(0)
            one(1)


def first_backward_body(pair, scales, *refs):
    blocks = refs[:6]
    x, act, slope, hidden, halves, grads, residual, saved = refs[6:]
    spread(blocks, residual, pair, True)

    def store(i, step, columns, value):
        grads[i, :, columns] = value.astype(BF16)

    gradients(residual, x, act, slope, hidden, halves.at[2], scales, saved, store, True)


def update_forward_body(pair, scale_model, *refs):
    core, base, grads, near_grads, x = refs[:5]
    kept, sent_in, sent_out = refs[5:10], refs[10], refs[11]
    partials, halves, turned = refs[12:18], refs[18], refs[19]
    size = sent_in.shape[0] * 2 // 3
    offset = core[0] * (halves.shape[1] - size)
    weights, act, slope, hidden, down = kept

    for i in range(3):

        @pl.loop(0, base.shape[1] // UNITS)
        def _(step):
            here = pl.ds(pl.multiple_of(step * UNITS, UNITS), UNITS)
            moved = grads[i, here, :].astype(F32) + near_grads[i, here, :].astype(F32)
            value = base[i, here, :] - (LEARNING_RATE * 0.5) * moved
            weights[i, here, :] = value
            halves[i, here, :] = value.astype(BF16)

    forward_into(x, halves, (act, slope, hidden), scale_model)
    partial_into(hidden, halves.at[2], partials, pair, False, turned)

    def keep(start):
        down[pl.ds(start, UNITS), :] = halves[2, pl.ds(start, UNITS), :]

    def send(start):
        source = pl.ds(pl.multiple_of(offset + start, PART), PART)
        sent_in[pl.ds(start, PART), :] = halves[0, source, :]
        sent_out[pl.ds(pl.multiple_of(size // 2 + start, PART), PART), :] = halves[2, source, :]

    def send_half(start):
        source = pl.ds(pl.multiple_of(offset + start, PART), PART)
        sent_in[pl.ds(pl.multiple_of(size + start, PART), PART), :] = halves[1, source, :]
        source = pl.ds(pl.multiple_of(offset + size // 2 + start, PART), PART)
        sent_out[pl.ds(start, PART), :] = halves[1, source, :]

    each_part(down.shape[0], UNITS, keep)
    each_part(size, PART, send)
    each_part(size // 2, PART, send_half)


def far_forward_body(scale_model, core, x, direct, beside, weights, act, slope, hidden):
    size = direct.shape[0] // 3
    last = weights.shape[1] - size
    first = core[0] * last

    def place(start):
        for i in range(3):
            source = pl.ds(pl.multiple_of(i * size + start, PART), PART)
            weights[i, pl.ds(pl.multiple_of(first + start, PART), PART), :] = direct[source, :]
            weights[i, pl.ds(pl.multiple_of(last - first + start, PART), PART), :] = beside[source, :]

    each_part(size, PART, place)
    forward_into(x, weights, (act, slope, hidden), scale_model)


def join_body(direct_in, direct_out, joined):
    def one(start):
        here = pl.ds(start, PART)
        joined[here, :] = direct_in[here, :]
        joined[pl.ds(pl.multiple_of(direct_in.shape[0] + start, PART), PART), :] = direct_out[here, :]

    each_part(direct_in.shape[0], PART, one)


def own_backward_body(pair, scales, *refs):
    blocks = refs[:6]
    x, act, slope, hidden, down, weights, total, residual, saved = refs[6:]
    spread(blocks, residual, pair, False)

    def store(i, step, columns, value):
        total[i, :, columns] = weights[i, :, columns] * 0.5 - (LEARNING_RATE * 0.5) * value

    gradients(residual, x, act, slope, hidden, down, scales, saved, store, True)


def last_body(pair, scales, *refs):
    blocks = refs[:6]
    x, act, slope, hidden, far, total, out_gate, out_up, out_down, residual, staged, sems, saved = refs[6:]
    outs = (out_gate, out_up, out_down)
    spread(blocks, residual, pair, False)

    def out_copy(i, step, columns):
        return pltpu.make_async_copy(
            staged.at[i, :, columns], outs[i].at[0, :, columns], sems.at[i, step]
        )

    def store(i, step, columns, value):
        mean = total[i, :, columns] + far[i, :, columns].astype(F32) * 0.5
        staged[i, :, columns] = mean - (LEARNING_RATE * 0.5) * value
        out_copy(i, step, columns).start()

    gradients(residual, x, act, slope, hidden, far.at[2], scales, saved, store, False)
    for i in (2, 0, 1):
        for step in range(x.shape[1] // COLUMNS):
            out_copy(i, step, slice(step * COLUMNS, (step + 1) * COLUMNS)).wait()


def local(tokens, targets, w_gate, w_up, w_down, *, n_rep, n_z, hidden_units):
    n_hid = 2 * n_z
    rows, width = tokens.shape[1], tokens.shape[2]
    pair = 2 * rows
    scale_model = float(width) ** (-0.5)
    scale_hidden = float(hidden_units) ** (-0.5)

    def along_z(value, shift):
        pairs = [(h, (h // n_z) * n_z + (h % n_z + shift) % n_z) for h in range(n_hid)]
        return lax.ppermute(value, "hid", pairs)

    def across_y(value):
        return lax.ppermute(value, "hid", [(h, h ^ n_z) for h in range(n_hid)])

    def with_replica(value, mask):
        return lax.ppermute(value, "rep", [(r, r ^ mask) for r in range(n_rep)])

    def two_along(value, sign):
        pairs = []
        for r in range(n_rep):
            step = sign * (n_z // 4) if r % 2 == 0 else -sign * (n_z // 4)
            for h in range(n_hid):
                to = (h // n_z) * n_z + (h % n_z + step) % n_z
                pairs.append((r * n_hid + h, r * n_hid + to))
        return lax.ppermute(value, ("rep", "hid"), pairs)

    def gather_far(block):
        return two_along(block, 1), two_along(block, -1)

    def gather_near(block, ahead, behind):
        across = two_along(ahead, 1)
        both = jnp.concatenate([ahead, behind], axis=0)
        left, right = along_z(both, 1), along_z(both, -1)
        return [block, ahead, behind, across, left, right]

    def gather_z(block):
        return gather_near(block, *gather_far(block))

    def reduce_z(partials):
        own, ahead, behind, across, left, right = partials
        own, ahead, behind = (v.astype(F32) for v in (own, ahead, behind))
        across = two_along(across, -1)
        left, right = along_z(left, -1), along_z(right, 1)
        ahead = ahead + left[:pair].astype(F32) + right[:pair].astype(F32) + across.astype(F32)
        behind = behind + left[pair:].astype(F32) + right[pair:].astype(F32)
        ahead, behind = two_along(ahead.astype(BF16), -1), two_along(behind.astype(BF16), 1)
        total = own + ahead.astype(F32) + behind.astype(F32)
        other = across_y(total.astype(BF16)).astype(F32)
        return total + jnp.concatenate([other[rows:], other[:rows]], axis=0)

    def residual_of(partials, target):
        output = reduce_z(partials) * scale_hidden
        return (output - target.astype(F32)).astype(BF16)

    units = w_gate.shape[1]
    count = n_z * pair
    product = 2 * units * count * width
    scales = (scale_model, scale_hidden)

    def arr(shape, dtype):
        return jax.ShapeDtypeStruct(shape, dtype)

    stack_f32, stack_bf16 = arr((3, units, width), F32), arr((3, units, width), BF16)
    acts = [arr((units, count), F32), arr((units, count), F32), arr((units, count), BF16)]
    travel = [arr((pair, width), BF16)] * 4 + [arr((2 * pair, width), BF16)] * 2
    tokens_shape = arr((count, width), BF16)
    grad_scratch = pltpu.VMEM((2, units, count), BF16)
    residual_scratch = pltpu.VMEM((count, width), BF16)
    turned_scratch = pltpu.VMEM((count, units), BF16)

    first = jnp.concatenate([tokens[0], across_y(tokens[0]), tokens[1]], axis=0)
    mine, halves = kernel_call(
        cast_body, [stack_f32, stack_bf16], (w_gate[0], w_up[0], w_down[0]), 0, LIMIT
    )
    near = with_replica(mine, 1)
    blocks = gather_z(first)

    x0, column, act, slope, hidden, *partials = kernel_call(
        functools.partial(first_forward_body, pair, scale_model),
        [tokens_shape, arr((n_z * rows + pair, width), BF16), *acts, *travel],
        (*blocks, targets, halves),
        3 * product,
        LIMIT,
        (turned_scratch,),
    )
    beside = across_y(column)
    half = n_z * rows
    x1 = jnp.concatenate([column[:half], beside[:half]], axis=0)
    target0, target1 = (
        jnp.concatenate([targets[i], beside[half + i * rows : half + (i + 1) * rows]], axis=0)
        for i in range(2)
    )

    blocks = gather_z(residual_of(partials, target0))
    x1_far = with_replica(x1, 2)
    (grads,) = kernel_call(
        functools.partial(first_backward_body, pair, scales),
        [stack_bf16],
        (*blocks, x0, act, slope, hidden, halves),
        4 * product,
        LIMIT,
        (residual_scratch, grad_scratch),
    )
    near_grads = with_replica(grads, 1)

    (base,) = kernel_call(mean_body, [stack_f32], (mine, near), 0, UPDATE_LIMIT)

    core = (lax.axis_index("rep") % 2).astype(jnp.int32).reshape(1)
    cut = -(-units // 32) * 16
    weights, act, slope, hidden, down, sent_in, sent_out, *partials = kernel_call(
        functools.partial(update_forward_body, pair, scale_model),
        [
            stack_f32,
            *acts,
            arr((units, width), BF16),
            arr((cut * 3 // 2, width), BF16),
            arr((cut * 3 // 2, width), BF16),
            *travel,
        ],
        (core, base, grads, near_grads, x1),
        3 * product,
        UPDATE_LIMIT,
        (
            pltpu.VMEM((3, units, width), BF16),
            turned_scratch,
        ),
        [SMEM_SPEC] + [VMEM_SPEC] * 4,
    )
    direct_in = with_replica(sent_in, 2)
    direct_out = with_replica(sent_out, 2)
    (direct,) = kernel_call(
        join_body, [arr((3 * cut, width), BF16)], (direct_in, direct_out), 0, 12
    )
    passed = with_replica(direct, 1)

    residual = residual_of(partials, target1)
    residual_far = with_replica(residual, 2)
    blocks = gather_z(residual)
    far_blocks = gather_z(residual_far)
    (total,) = kernel_call(
        functools.partial(own_backward_body, pair, scales),
        [stack_f32],
        (*blocks, x1, act, slope, hidden, down, weights),
        4 * product,
        LIMIT,
        (residual_scratch, grad_scratch),
    )
    far, act, slope, hidden = kernel_call(
        functools.partial(far_forward_body, scale_model),
        [stack_bf16, *acts],
        (core, x1_far, direct, passed),
        2 * product,
        LIMIT,
        (),
        [SMEM_SPEC] + [VMEM_SPEC] * 3,
    )
    return kernel_call(
        functools.partial(last_body, pair, scales),
        [arr((1, units, width), F32)] * 3,
        (*far_blocks, x1_far, act, slope, hidden, far, total),
        4 * product,
        LIMIT,
        (
            residual_scratch,
            pltpu.VMEM((3, units, width), F32),
            pltpu.SemaphoreType.DMA((3, width // COLUMNS)),
            grad_scratch,
        ),
        None,
        [pl.BlockSpec(memory_space=pl.ANY)] * 3,
    )


def solution(mesh):
    n_rep, n_hid = mesh.shape["rep"], mesh.shape["hid"]
    hid_spec = P("rep", "hid", None)
    token_spec = P(None, ("rep", "hid"), None)

    def whole(tokens, targets, w_gate, w_up, w_down):
        def body(*args):
            return local(*args, n_rep=n_rep, n_z=n_hid // 2, hidden_units=w_gate.shape[1])

        return jax.shard_map(
            body,
            mesh=mesh,
            in_specs=(token_spec, token_spec, hid_spec, hid_spec, hid_spec),
            out_specs=(hid_spec, hid_spec, hid_spec),
            check_vma=False,
        )(tokens, targets, w_gate, w_up, w_down)

    return whole
```

```python
import functools

import jax
import jax.numpy as jnp
from jax import lax
from jax.experimental import pallas as pl
from jax.experimental.pallas import tpu as pltpu
from jax.sharding import PartitionSpec as P

LEARNING_RATE = 0.5
SQRT_2_PI = 0.7978845608028654
CUBIC = 0.044715
LIMIT = 12
UPDATE_LIMIT = 14
BF16, F32 = jnp.bfloat16, jnp.float32


def dot_nt(left, right):
    return lax.dot_general(left, right, (((1,), (1,)), ((), ())), preferred_element_type=F32)


def dot_nn(left, right):
    return lax.dot_general(left, right, (((1,), (0,)), ((), ())), preferred_element_type=F32)


def gelu_and_slope(value):
    inner = SQRT_2_PI * (value + CUBIC * value * value * value)
    tanh = jnp.tanh(inner)
    half = 0.5 * (1.0 + tanh)
    slope = half + 0.5 * value * (1.0 - tanh * tanh) * SQRT_2_PI * (1.0 + 3.0 * CUBIC * value * value)
    return value * half, slope


VMEM_SPEC = pl.BlockSpec(memory_space=pltpu.VMEM)
SMEM_SPEC = pl.BlockSpec(memory_space=pltpu.SMEM)
HBM_SPEC = pl.BlockSpec(memory_space=pltpu.HBM)


def kernel_call(body, out_shape, args, flops, limit, scratch=(), in_specs=None, out_specs=None, alias=None):
    size = sum(v.size * v.dtype.itemsize for v in args)
    size += sum(v.size * v.dtype.itemsize for v in out_shape)
    return pl.pallas_call(
        body,
        out_shape=out_shape,
        in_specs=[VMEM_SPEC] * len(args) if in_specs is None else in_specs,
        out_specs=[VMEM_SPEC] * len(out_shape) if out_specs is None else out_specs,
        scratch_shapes=list(scratch),
        cost_estimate=pl.CostEstimate(flops=flops, bytes_accessed=size, transcendentals=0),
        compiler_params=pltpu.CompilerParams(vmem_limit_bytes=limit * 2**20),
        input_output_aliases=alias or {},
    )(*args)


def pieces(k, pair, paired, total):
    if paired:
        return ((k * pair, 0, pair),)
    half = pair // 2
    return ((k * half, 0, half), (total // 2 + k * half, half, half))


def spread(refs, target, pair, paired):
    total = target.shape[0]
    k = 0
    for ref in refs:
        for i in range(ref.shape[0] // pair):
            for start, offset, size in pieces(k, pair, paired, total):
                target[start : start + size, :] = ref[i * pair + offset : i * pair + offset + size, :]
            k += 1


COLUMNS = 384
TOKENS = 256
UNITS = 48
PART = 16


def forward_into(x, weights, saved, scale_model):
    act_ref, slope_ref, hidden_ref = saved

    @pl.loop(0, x.shape[0] // TOKENS)
    def _(step):
        start = pl.multiple_of(step * TOKENS, TOKENS)
        here = pl.ds(start, TOKENS)
        batch = x[here, :]
        gate = dot_nt(weights[0], batch) * scale_model
        up = dot_nt(weights[1], batch) * scale_model
        act, slope = gelu_and_slope(gate)
        act_ref[:, here] = act
        slope_ref[:, here] = slope * up
        hidden_ref[:, here] = (act * up).astype(BF16)


def partial_into(hidden, down, refs, pair, paired, turned):
    total = hidden.shape[1]
    turned[...] = hidden[...].T

    @pl.loop(0, down.shape[1] // COLUMNS)
    def _(step):
        here = pl.ds(pl.multiple_of(step * COLUMNS, COLUMNS), COLUMNS)
        part = dot_nn(turned[...], down[:, here]).astype(BF16)
        k = 0
        for ref in refs:
            for i in range(ref.shape[0] // pair):
                for start, offset, size in pieces(k, pair, paired, total):
                    ref[i * pair + offset : i * pair + offset + size, here] = part[
                        start : start + size
                    ]
                k += 1


def each_part(total, size, body):
    @pl.loop(0, total // size)
    def _(step):
        body(pl.multiple_of(step * size, size))


def cast_body(gate, up, down, stacked, halves):
    def one(start):
        here = pl.ds(start, UNITS)
        for i, ref in enumerate((gate, up, down)):
            stacked[i, here, :] = ref[here, :]
            halves[i, here, :] = ref[here, :].astype(BF16)

    each_part(gate.shape[0], UNITS, one)


def mean_body(mine, near, base):
    for i in range(3):

        @pl.loop(0, mine.shape[1] // UNITS)
        def _(step):
            here = pl.ds(pl.multiple_of(step * UNITS, UNITS), UNITS)
            base[i, here, :] = (mine[i, here, :] + near[i, here, :]) * 0.5


def first_forward_body(pair, scale_model, *refs):
    blocks, targets, halves = refs[:6], refs[6], refs[7]
    x, column, act, slope, hidden = refs[8:13]
    partials, turned = refs[13:19], refs[19]
    rows = pair // 2
    size = pair + rows
    k = 0
    for ref in blocks:
        for i in range(ref.shape[0] // size):
            x[k * pair : (k + 1) * pair, :] = ref[i * size : i * size + pair, :]
            column[k * rows : (k + 1) * rows, :] = ref[i * size + pair : (i + 1) * size, :]
            k += 1
    column[k * rows : (k + 1) * rows, :] = targets[0]
    column[(k + 1) * rows :, :] = targets[1]
    forward_into(x, halves, (act, slope, hidden), scale_model)
    partial_into(hidden, halves.at[2], partials, pair, True, turned)


def gradients(x, act, slope, hidden, down, scales, lefts, rights, store):
    scale_model, scale_hidden = scales

    def copy(start):
        here = pl.ds(start, PART)
        rights[0, here, :] = x[here, :]

    def copy_hidden(start):
        here = pl.ds(start, PART)
        lefts[2, here, :] = hidden[here, :]

    each_part(x.shape[0], PART, copy)
    each_part(hidden.shape[0], PART, copy_hidden)

    @pl.loop(0, x.shape[0] // TOKENS)
    def _(step):
        here = pl.ds(pl.multiple_of(step * TOKENS, TOKENS), TOKENS)
        hidden_grad = dot_nt(down[...], rights[1, here, :]) * scale_hidden
        lefts[0, :, here] = (hidden_grad * slope[:, here]).astype(BF16)
        lefts[1, :, here] = (hidden_grad * act[:, here]).astype(BF16)

    @pl.loop(0, 3)
    def _(i):
        scale = jnp.where(i == 2, scale_hidden, scale_model)
        store(i, dot_nn(lefts[i], rights[i // 2]) * scale)


def first_backward_body(pair, scales, *refs):
    blocks = refs[:6]
    x, act, slope, hidden, halves, grads, lefts, rights = refs[6:]
    spread(blocks, rights.at[1], pair, True)

    def store(i, value):
        grads[i] = value.astype(BF16)

    gradients(x, act, slope, hidden, halves.at[2], scales, lefts, rights, store)


def update_forward_body(pair, scale_model, *refs):
    core, base, grads, near_grads, x = refs[:5]
    kept, sent_in, sent_out = refs[5:10], refs[10], refs[11]
    partials, halves, turned = refs[12:18], refs[18], refs[19]
    size = sent_in.shape[0] * 2 // 3
    offset = core[0] * (halves.shape[1] - size)
    weights, act, slope, hidden, down = kept

    for i in range(3):

        @pl.loop(0, base.shape[1] // UNITS)
        def _(step):
            here = pl.ds(pl.multiple_of(step * UNITS, UNITS), UNITS)
            moved = grads[i, here, :].astype(F32) + near_grads[i, here, :].astype(F32)
            value = base[i, here, :] - (LEARNING_RATE * 0.5) * moved
            weights[i, here, :] = value
            halves[i, here, :] = value.astype(BF16)

    forward_into(x, halves, (act, slope, hidden), scale_model)
    partial_into(hidden, halves.at[2], partials, pair, False, turned)

    def keep(start):
        down[pl.ds(start, UNITS), :] = halves[2, pl.ds(start, UNITS), :]

    def send(start):
        source = pl.ds(pl.multiple_of(offset + start, PART), PART)
        sent_in[pl.ds(start, PART), :] = halves[0, source, :]
        sent_out[pl.ds(pl.multiple_of(size // 2 + start, PART), PART), :] = halves[2, source, :]

    def send_half(start):
        source = pl.ds(pl.multiple_of(offset + start, PART), PART)
        sent_in[pl.ds(pl.multiple_of(size + start, PART), PART), :] = halves[1, source, :]
        source = pl.ds(pl.multiple_of(offset + size // 2 + start, PART), PART)
        sent_out[pl.ds(start, PART), :] = halves[1, source, :]

    each_part(down.shape[0], UNITS, keep)
    each_part(size, PART, send)
    each_part(size // 2, PART, send_half)


def far_forward_body(scale_model, core, x, direct, beside, weights, act, slope, hidden):
    size = direct.shape[0] // 3
    last = weights.shape[1] - size
    first = core[0] * last

    def place(start):
        for i in range(3):
            source = pl.ds(pl.multiple_of(i * size + start, PART), PART)
            weights[i, pl.ds(pl.multiple_of(first + start, PART), PART), :] = direct[source, :]
            weights[i, pl.ds(pl.multiple_of(last - first + start, PART), PART), :] = beside[source, :]

    each_part(size, PART, place)
    forward_into(x, weights, (act, slope, hidden), scale_model)


def join_body(direct_in, direct_out, joined):
    def one(start):
        here = pl.ds(start, PART)
        joined[here, :] = direct_in[here, :]
        joined[pl.ds(pl.multiple_of(direct_in.shape[0] + start, PART), PART), :] = direct_out[here, :]

    each_part(direct_in.shape[0], PART, one)


def own_backward_body(pair, scales, *refs):
    blocks = refs[:6]
    x, act, slope, hidden, down, weights, total, lefts, rights = refs[6:]
    spread(blocks, rights.at[1], pair, False)

    def store(i, value):
        total[i] = weights[i] * 0.5 - (LEARNING_RATE * 0.5) * value

    gradients(x, act, slope, hidden, down, scales, lefts, rights, store)


def last_body(pair, scales, *refs):
    blocks = refs[:6]
    x, act, slope, hidden, far, total, out_gate, out_up, out_down, staged, sems, lefts, rights = refs[6:]
    spread(blocks, rights.at[1], pair, False)
    copies = [
        pltpu.make_async_copy(staged.at[i], out.at[0], sems.at[i])
        for i, out in enumerate((out_gate, out_up, out_down))
    ]

    def store(i, value):
        mean = total[i] + far[i].astype(F32) * 0.5
        staged[i] = mean - (LEARNING_RATE * 0.5) * value
        for k, copy in enumerate(copies):
            pl.when(i == k)(copy.start)

    gradients(x, act, slope, hidden, far.at[2], scales, lefts, rights, store)
    for copy in copies:
        copy.wait()


def local(tokens, targets, w_gate, w_up, w_down, *, n_rep, n_z, hidden_units):
    n_hid = 2 * n_z
    rows, width = tokens.shape[1], tokens.shape[2]
    pair = 2 * rows
    scale_model = float(width) ** (-0.5)
    scale_hidden = float(hidden_units) ** (-0.5)

    def along_z(value, shift):
        pairs = [(h, (h // n_z) * n_z + (h % n_z + shift) % n_z) for h in range(n_hid)]
        return lax.ppermute(value, "hid", pairs)

    def across_y(value):
        return lax.ppermute(value, "hid", [(h, h ^ n_z) for h in range(n_hid)])

    def with_replica(value, mask):
        return lax.ppermute(value, "rep", [(r, r ^ mask) for r in range(n_rep)])

    def two_along(value, sign):
        pairs = []
        for r in range(n_rep):
            step = sign * (n_z // 4) if r % 2 == 0 else -sign * (n_z // 4)
            for h in range(n_hid):
                to = (h // n_z) * n_z + (h % n_z + step) % n_z
                pairs.append((r * n_hid + h, r * n_hid + to))
        return lax.ppermute(value, ("rep", "hid"), pairs)

    def gather_far(block):
        return two_along(block, 1), two_along(block, -1)

    def gather_near(block, ahead, behind):
        across = two_along(ahead, 1)
        both = jnp.concatenate([ahead, behind], axis=0)
        left, right = along_z(both, 1), along_z(both, -1)
        return [block, ahead, behind, across, left, right]

    def gather_z(block):
        return gather_near(block, *gather_far(block))

    def reduce_z(partials):
        own, ahead, behind, across, left, right = partials
        own, ahead, behind = (v.astype(F32) for v in (own, ahead, behind))
        across = two_along(across, -1)
        left, right = along_z(left, -1), along_z(right, 1)
        ahead = ahead + left[:pair].astype(F32) + right[:pair].astype(F32) + across.astype(F32)
        behind = behind + left[pair:].astype(F32) + right[pair:].astype(F32)
        ahead, behind = two_along(ahead.astype(BF16), -1), two_along(behind.astype(BF16), 1)
        total = own + ahead.astype(F32) + behind.astype(F32)
        other = across_y(total.astype(BF16)).astype(F32)
        return total + jnp.concatenate([other[rows:], other[:rows]], axis=0)

    def residual_of(partials, target):
        output = reduce_z(partials) * scale_hidden
        return (output - target.astype(F32)).astype(BF16)

    units = w_gate.shape[1]
    count = n_z * pair
    product = 2 * units * count * width
    scales = (scale_model, scale_hidden)

    def arr(shape, dtype):
        return jax.ShapeDtypeStruct(shape, dtype)

    stack_f32, stack_bf16 = arr((3, units, width), F32), arr((3, units, width), BF16)
    acts = [arr((units, count), F32), arr((units, count), F32), arr((units, count), BF16)]
    travel = [arr((pair, width), BF16)] * 4 + [arr((2 * pair, width), BF16)] * 2
    tokens_shape = arr((count, width), BF16)
    grad_scratch = (pltpu.VMEM((3, units, count), BF16), pltpu.VMEM((2, count, width), BF16))
    turned_scratch = pltpu.VMEM((count, units), BF16)

    first = jnp.concatenate([tokens[0], across_y(tokens[0]), tokens[1]], axis=0)
    mine, halves = kernel_call(
        cast_body, [stack_f32, stack_bf16], (w_gate[0], w_up[0], w_down[0]), 0, LIMIT
    )
    near = with_replica(mine, 1)
    blocks = gather_z(first)

    x0, column, act, slope, hidden, *partials = kernel_call(
        functools.partial(first_forward_body, pair, scale_model),
        [tokens_shape, arr((n_z * rows + pair, width), BF16), *acts, *travel],
        (*blocks, targets, halves),
        3 * product,
        LIMIT,
        (turned_scratch,),
    )
    beside = across_y(column)
    half = n_z * rows
    x1 = jnp.concatenate([column[:half], beside[:half]], axis=0)
    target0, target1 = (
        jnp.concatenate([targets[i], beside[half + i * rows : half + (i + 1) * rows]], axis=0)
        for i in range(2)
    )

    blocks = gather_z(residual_of(partials, target0))
    x1_far = with_replica(x1, 2)
    (grads,) = kernel_call(
        functools.partial(first_backward_body, pair, scales),
        [stack_bf16],
        (*blocks, x0, act, slope, hidden, halves),
        4 * product,
        LIMIT,
        grad_scratch,
    )
    near_grads = with_replica(grads, 1)

    (base,) = kernel_call(mean_body, [stack_f32], (mine, near), 0, UPDATE_LIMIT)

    core = (lax.axis_index("rep") % 2).astype(jnp.int32).reshape(1)
    cut = -(-units // 32) * 16
    weights, act, slope, hidden, down, sent_in, sent_out, *partials = kernel_call(
        functools.partial(update_forward_body, pair, scale_model),
        [
            stack_f32,
            *acts,
            arr((units, width), BF16),
            arr((cut * 3 // 2, width), BF16),
            arr((cut * 3 // 2, width), BF16),
            *travel,
        ],
        (core, base, grads, near_grads, x1),
        3 * product,
        UPDATE_LIMIT,
        (
            pltpu.VMEM((3, units, width), BF16),
            turned_scratch,
        ),
        [SMEM_SPEC] + [VMEM_SPEC] * 4,
    )
    direct_in = with_replica(sent_in, 2)
    direct_out = with_replica(sent_out, 2)
    (direct,) = kernel_call(
        join_body, [arr((3 * cut, width), BF16)], (direct_in, direct_out), 0, 12
    )
    passed = with_replica(direct, 1)

    residual = residual_of(partials, target1)
    residual_far = with_replica(residual, 2)
    blocks = gather_z(residual)
    far_blocks = gather_z(residual_far)
    (total,) = kernel_call(
        functools.partial(own_backward_body, pair, scales),
        [stack_f32],
        (*blocks, x1, act, slope, hidden, down, weights),
        4 * product,
        LIMIT,
        grad_scratch,
    )
    far, act, slope, hidden = kernel_call(
        functools.partial(far_forward_body, scale_model),
        [stack_bf16, *acts],
        (core, x1_far, direct, passed),
        2 * product,
        LIMIT,
        (),
        [SMEM_SPEC] + [VMEM_SPEC] * 3,
    )
    return kernel_call(
        functools.partial(last_body, pair, scales),
        [arr((1, units, width), F32)] * 3,
        (*far_blocks, x1_far, act, slope, hidden, far, total),
        4 * product,
        LIMIT,
        (
            pltpu.VMEM((3, units, width), F32),
            pltpu.SemaphoreType.DMA((3,)),
            *grad_scratch,
        ),
        None,
        [pl.BlockSpec(memory_space=pl.ANY)] * 3,
    )


def solution(mesh):
    n_rep, n_hid = mesh.shape["rep"], mesh.shape["hid"]
    hid_spec = P("rep", "hid", None)
    token_spec = P(None, ("rep", "hid"), None)

    def whole(tokens, targets, w_gate, w_up, w_down):
        def body(*args):
            return local(*args, n_rep=n_rep, n_z=n_hid // 2, hidden_units=w_gate.shape[1])

        return jax.shard_map(
            body,
            mesh=mesh,
            in_specs=(token_spec, token_spec, hid_spec, hid_spec, hid_spec),
            out_specs=(hid_spec, hid_spec, hid_spec),
            check_vma=False,
        )(tokens, targets, w_gate, w_up, w_down)

    return whole
```

```python
import functools

import jax
import jax.numpy as jnp
from jax import lax
from jax.experimental import pallas as pl
from jax.experimental.pallas import tpu as pltpu
from jax.sharding import PartitionSpec as P

LEARNING_RATE = 0.5
SQRT_2_PI = 0.7978845608028654
CUBIC = 0.044715
LIMIT = 12
UPDATE_LIMIT = 14
BF16, F32 = jnp.bfloat16, jnp.float32


def dot_nt(left, right):
    return lax.dot_general(left, right, (((1,), (1,)), ((), ())), preferred_element_type=F32)


def dot_nn(left, right):
    return lax.dot_general(left, right, (((1,), (0,)), ((), ())), preferred_element_type=F32)


def gelu_and_slope(value):
    inner = SQRT_2_PI * (value + CUBIC * value * value * value)
    tanh = jnp.tanh(inner)
    half = 0.5 * (1.0 + tanh)
    slope = half + 0.5 * value * (1.0 - tanh * tanh) * SQRT_2_PI * (1.0 + 3.0 * CUBIC * value * value)
    return value * half, slope


VMEM_SPEC = pl.BlockSpec(memory_space=pltpu.VMEM)
SMEM_SPEC = pl.BlockSpec(memory_space=pltpu.SMEM)
HBM_SPEC = pl.BlockSpec(memory_space=pltpu.HBM)


def kernel_call(body, out_shape, args, flops, limit, scratch=(), in_specs=None, out_specs=None, alias=None):
    size = sum(v.size * v.dtype.itemsize for v in args)
    size += sum(v.size * v.dtype.itemsize for v in out_shape)
    return pl.pallas_call(
        body,
        out_shape=out_shape,
        in_specs=[VMEM_SPEC] * len(args) if in_specs is None else in_specs,
        out_specs=[VMEM_SPEC] * len(out_shape) if out_specs is None else out_specs,
        scratch_shapes=list(scratch),
        cost_estimate=pl.CostEstimate(flops=flops, bytes_accessed=size, transcendentals=0),
        compiler_params=pltpu.CompilerParams(vmem_limit_bytes=limit * 2**20),
        input_output_aliases=alias or {},
    )(*args)


def pieces(k, pair, paired, total):
    if paired:
        return ((k * pair, 0, pair),)
    half = pair // 2
    return ((k * half, 0, half), (total // 2 + k * half, half, half))


def spread(refs, target, pair, paired):
    total = target.shape[0]
    k = 0
    for ref in refs:
        for i in range(ref.shape[0] // pair):

            def copy(part, ref=ref, i=i, k=k):
                for start, offset, size in pieces(k, pair, paired, total):
                    for at in range(0, size, pair // 2):
                        source = pl.ds(pl.multiple_of(i * pair + offset + at + part, PART), PART)
                        here = pl.ds(pl.multiple_of(start + at + part, PART), PART)
                        target[here, :] = ref[source, :]

            each_part(pair // 2, PART, copy)
            k += 1


COLUMNS = 384
TOKENS = 256
UNITS = 48
PART = 16


def forward_into(x, weights, saved, scale_model):
    act_ref, slope_ref, hidden_ref = saved

    @pl.loop(0, x.shape[0] // TOKENS)
    def _(step):
        start = pl.multiple_of(step * TOKENS, TOKENS)
        here = pl.ds(start, TOKENS)
        batch = x[here, :]
        gate = dot_nt(weights[0], batch) * scale_model
        up = dot_nt(weights[1], batch) * scale_model
        act, slope = gelu_and_slope(gate)
        act_ref[:, here] = act
        slope_ref[:, here] = slope * up
        hidden_ref[:, here] = (act * up).astype(BF16)


def partial_into(hidden, down, refs, pair, paired, turned):
    total = hidden.shape[1]
    turned[...] = hidden[...].T

    @pl.loop(0, down.shape[1] // COLUMNS)
    def _(step):
        here = pl.ds(pl.multiple_of(step * COLUMNS, COLUMNS), COLUMNS)
        part = dot_nn(turned[...], down[:, here]).astype(BF16)
        k = 0
        for ref in refs:
            for i in range(ref.shape[0] // pair):
                for start, offset, size in pieces(k, pair, paired, total):
                    ref[i * pair + offset : i * pair + offset + size, here] = part[
                        start : start + size
                    ]
                k += 1


def each_part(total, size, body):
    @pl.loop(0, total // size)
    def _(step):
        body(pl.multiple_of(step * size, size))


def cast_body(gate, up, down, stacked, halves):
    def one(start):
        here = pl.ds(start, PART)
        for i, ref in enumerate((gate, up, down)):
            stacked[i, here, :] = ref[here, :]
            halves[i, here, :] = ref[here, :].astype(BF16)

    each_part(gate.shape[0], PART, one)


def mean_body(mine, near, base):
    @pl.loop(0, 3)
    def _(i):
        @pl.loop(0, mine.shape[1] // UNITS)
        def _(step):
            here = pl.ds(pl.multiple_of(step * UNITS, UNITS), UNITS)
            base[i, here, :] = (mine[i, here, :] + near[i, here, :]) * 0.5


def first_forward_body(pair, scale_model, *refs):
    blocks, targets, halves = refs[:6], refs[6], refs[7]
    x, column, act, slope, hidden = refs[8:13]
    partials, turned = refs[13:19], refs[19]
    rows = pair // 2
    size = pair + rows
    k = 0
    for ref in blocks:
        for i in range(ref.shape[0] // size):

            def copy(part, ref=ref, i=i, k=k):
                for at, target, start in (
                    (0, x, k * pair),
                    (rows, x, k * pair + rows),
                    (pair, column, k * rows),
                ):
                    source = pl.ds(pl.multiple_of(i * size + at + part, PART), PART)
                    here = pl.ds(pl.multiple_of(start + part, PART), PART)
                    target[here, :] = ref[source, :]

            each_part(rows, PART, copy)
            k += 1
    column[k * rows : (k + 1) * rows, :] = targets[0]
    column[(k + 1) * rows :, :] = targets[1]
    forward_into(x, halves, (act, slope, hidden), scale_model)
    partial_into(hidden, halves.at[2], partials, pair, True, turned)


def gradients(x, act, slope, hidden, down, scales, lefts, rights, store):
    scale_model, scale_hidden = scales

    def copy(start):
        here = pl.ds(start, PART)
        rights[0, here, :] = x[here, :]

    def copy_hidden(start):
        here = pl.ds(start, PART)
        lefts[2, here, :] = hidden[here, :]

    each_part(x.shape[0], PART, copy)
    each_part(hidden.shape[0], PART, copy_hidden)

    @pl.loop(0, x.shape[0] // TOKENS)
    def _(step):
        here = pl.ds(pl.multiple_of(step * TOKENS, TOKENS), TOKENS)
        hidden_grad = dot_nt(down[...], rights[1, here, :]) * scale_hidden
        lefts[0, :, here] = (hidden_grad * slope[:, here]).astype(BF16)
        lefts[1, :, here] = (hidden_grad * act[:, here]).astype(BF16)

    @pl.loop(0, 3)
    def _(i):
        scale = jnp.where(i == 2, scale_hidden, scale_model)
        store(i, dot_nn(lefts[i], rights[i // 2]) * scale)


def first_backward_body(pair, scales, *refs):
    blocks = refs[:6]
    x, act, slope, hidden, halves, grads, lefts, rights = refs[6:]
    spread(blocks, rights.at[1], pair, True)

    def store(i, value):
        grads[i] = value.astype(BF16)

    gradients(x, act, slope, hidden, halves.at[2], scales, lefts, rights, store)


def update_forward_body(pair, scale_model, *refs):
    core, base, grads, near_grads, x = refs[:5]
    kept, sent_in, sent_out = refs[5:10], refs[10], refs[11]
    partials, halves, turned = refs[12:18], refs[18], refs[19]
    size = sent_in.shape[0] * 2 // 3
    offset = core[0] * (halves.shape[1] - size)
    weights, act, slope, hidden, down = kept

    @pl.loop(0, 3)
    def _(i):
        @pl.loop(0, base.shape[1] // UNITS)
        def _(step):
            here = pl.ds(pl.multiple_of(step * UNITS, UNITS), UNITS)
            moved = grads[i, here, :].astype(F32) + near_grads[i, here, :].astype(F32)
            value = base[i, here, :] - (LEARNING_RATE * 0.5) * moved
            weights[i, here, :] = value
            halves[i, here, :] = value.astype(BF16)

    forward_into(x, halves, (act, slope, hidden), scale_model)
    partial_into(hidden, halves.at[2], partials, pair, False, turned)

    def keep(start):
        down[pl.ds(start, PART), :] = halves[2, pl.ds(start, PART), :]

    def send(start):
        source = pl.ds(pl.multiple_of(offset + start, PART), PART)
        sent_in[pl.ds(start, PART), :] = halves[0, source, :]
        sent_out[pl.ds(pl.multiple_of(size // 2 + start, PART), PART), :] = halves[2, source, :]

    def send_half(start):
        source = pl.ds(pl.multiple_of(offset + start, PART), PART)
        sent_in[pl.ds(pl.multiple_of(size + start, PART), PART), :] = halves[1, source, :]
        source = pl.ds(pl.multiple_of(offset + size // 2 + start, PART), PART)
        sent_out[pl.ds(start, PART), :] = halves[1, source, :]

    each_part(down.shape[0], PART, keep)
    each_part(size, PART, send)
    each_part(size // 2, PART, send_half)


def far_forward_body(scale_model, core, x, direct, beside, weights, act, slope, hidden):
    size = direct.shape[0] // 3
    last = weights.shape[1] - size
    first = core[0] * last

    def place(start):
        for i in range(3):
            source = pl.ds(pl.multiple_of(i * size + start, PART), PART)
            weights[i, pl.ds(pl.multiple_of(first + start, PART), PART), :] = direct[source, :]
            weights[i, pl.ds(pl.multiple_of(last - first + start, PART), PART), :] = beside[source, :]

    each_part(size, PART, place)
    forward_into(x, weights, (act, slope, hidden), scale_model)


def join_body(direct_in, direct_out, joined):
    def one(start):
        here = pl.ds(start, PART)
        joined[here, :] = direct_in[here, :]
        joined[pl.ds(pl.multiple_of(direct_in.shape[0] + start, PART), PART), :] = direct_out[here, :]

    each_part(direct_in.shape[0], PART, one)


def own_backward_body(pair, scales, *refs):
    blocks = refs[:6]
    x, act, slope, hidden, down, weights, total, lefts, rights = refs[6:]
    spread(blocks, rights.at[1], pair, False)

    def store(i, value):
        total[i] = weights[i] * 0.5 - (LEARNING_RATE * 0.5) * value

    gradients(x, act, slope, hidden, down, scales, lefts, rights, store)


def last_body(pair, scales, *refs):
    blocks = refs[:6]
    x, act, slope, hidden, far, total, out_gate, out_up, out_down, staged, sems, lefts, rights = refs[6:]
    spread(blocks, rights.at[1], pair, False)
    copies = [
        pltpu.make_async_copy(staged.at[i], out.at[0], sems.at[i])
        for i, out in enumerate((out_gate, out_up, out_down))
    ]

    def store(i, value):
        mean = total[i] + far[i].astype(F32) * 0.5
        staged[i] = mean - (LEARNING_RATE * 0.5) * value
        for k, copy in enumerate(copies):
            pl.when(i == k)(copy.start)

    gradients(x, act, slope, hidden, far.at[2], scales, lefts, rights, store)
    for copy in copies:
        copy.wait()


def local(tokens, targets, w_gate, w_up, w_down, *, n_rep, n_z, hidden_units):
    n_hid = 2 * n_z
    rows, width = tokens.shape[1], tokens.shape[2]
    pair = 2 * rows
    scale_model = float(width) ** (-0.5)
    scale_hidden = float(hidden_units) ** (-0.5)

    def along_z(value, shift):
        pairs = [(h, (h // n_z) * n_z + (h % n_z + shift) % n_z) for h in range(n_hid)]
        return lax.ppermute(value, "hid", pairs)

    def across_y(value):
        return lax.ppermute(value, "hid", [(h, h ^ n_z) for h in range(n_hid)])

    def with_replica(value, mask):
        return lax.ppermute(value, "rep", [(r, r ^ mask) for r in range(n_rep)])

    def two_along(value, sign):
        pairs = []
        for r in range(n_rep):
            step = sign * (n_z // 4) if r % 2 == 0 else -sign * (n_z // 4)
            for h in range(n_hid):
                to = (h // n_z) * n_z + (h % n_z + step) % n_z
                pairs.append((r * n_hid + h, r * n_hid + to))
        return lax.ppermute(value, ("rep", "hid"), pairs)

    def gather_far(block):
        return two_along(block, 1), two_along(block, -1)

    def gather_near(block, ahead, behind):
        across = two_along(ahead, 1)
        both = jnp.concatenate([ahead, behind], axis=0)
        left, right = along_z(both, 1), along_z(both, -1)
        return [block, ahead, behind, across, left, right]

    def gather_z(block):
        return gather_near(block, *gather_far(block))

    def reduce_z(partials):
        own, ahead, behind, across, left, right = partials
        own, ahead, behind = (v.astype(F32) for v in (own, ahead, behind))
        across = two_along(across, -1)
        left, right = along_z(left, -1), along_z(right, 1)
        ahead = ahead + left[:pair].astype(F32) + right[:pair].astype(F32) + across.astype(F32)
        behind = behind + left[pair:].astype(F32) + right[pair:].astype(F32)
        ahead, behind = two_along(ahead.astype(BF16), -1), two_along(behind.astype(BF16), 1)
        total = own + ahead.astype(F32) + behind.astype(F32)
        other = across_y(total.astype(BF16)).astype(F32)
        return total + jnp.concatenate([other[rows:], other[:rows]], axis=0)

    def residual_of(partials, target):
        output = reduce_z(partials) * scale_hidden
        return (output - target.astype(F32)).astype(BF16)

    units = w_gate.shape[1]
    count = n_z * pair
    product = 2 * units * count * width
    scales = (scale_model, scale_hidden)

    def arr(shape, dtype):
        return jax.ShapeDtypeStruct(shape, dtype)

    stack_f32, stack_bf16 = arr((3, units, width), F32), arr((3, units, width), BF16)
    acts = [arr((units, count), F32), arr((units, count), F32), arr((units, count), BF16)]
    travel = [arr((pair, width), BF16)] * 4 + [arr((2 * pair, width), BF16)] * 2
    tokens_shape = arr((count, width), BF16)
    grad_scratch = (pltpu.VMEM((3, units, count), BF16), pltpu.VMEM((2, count, width), BF16))
    turned_scratch = pltpu.VMEM((count, units), BF16)

    first = jnp.concatenate([tokens[0], across_y(tokens[0]), tokens[1]], axis=0)
    mine, halves = kernel_call(
        cast_body, [stack_f32, stack_bf16], (w_gate[0], w_up[0], w_down[0]), 0, LIMIT
    )
    near = with_replica(mine, 1)
    blocks = gather_z(first)

    x0, column, act, slope, hidden, *partials = kernel_call(
        functools.partial(first_forward_body, pair, scale_model),
        [tokens_shape, arr((n_z * rows + pair, width), BF16), *acts, *travel],
        (*blocks, targets, halves),
        3 * product,
        LIMIT,
        (turned_scratch,),
    )
    beside = across_y(column)
    half = n_z * rows
    x1 = jnp.concatenate([column[:half], beside[:half]], axis=0)
    target0, target1 = (
        jnp.concatenate([targets[i], beside[half + i * rows : half + (i + 1) * rows]], axis=0)
        for i in range(2)
    )

    blocks = gather_z(residual_of(partials, target0))
    x1_far = with_replica(x1, 2)
    (grads,) = kernel_call(
        functools.partial(first_backward_body, pair, scales),
        [stack_bf16],
        (*blocks, x0, act, slope, hidden, halves),
        4 * product,
        LIMIT,
        grad_scratch,
    )
    near_grads = with_replica(grads, 1)

    (base,) = kernel_call(mean_body, [stack_f32], (mine, near), 0, UPDATE_LIMIT)

    core = (lax.axis_index("rep") % 2).astype(jnp.int32).reshape(1)
    cut = -(-units // 32) * 16
    weights, act, slope, hidden, down, sent_in, sent_out, *partials = kernel_call(
        functools.partial(update_forward_body, pair, scale_model),
        [
            stack_f32,
            *acts,
            arr((units, width), BF16),
            arr((cut * 3 // 2, width), BF16),
            arr((cut * 3 // 2, width), BF16),
            *travel,
        ],
        (core, base, grads, near_grads, x1),
        3 * product,
        UPDATE_LIMIT,
        (
            pltpu.VMEM((3, units, width), BF16),
            turned_scratch,
        ),
        [SMEM_SPEC] + [VMEM_SPEC] * 4,
    )
    direct_in = with_replica(sent_in, 2)
    direct_out = with_replica(sent_out, 2)
    (direct,) = kernel_call(
        join_body, [arr((3 * cut, width), BF16)], (direct_in, direct_out), 0, 12
    )
    passed = with_replica(direct, 1)

    residual = residual_of(partials, target1)
    residual_far = with_replica(residual, 2)
    blocks = gather_z(residual)
    far_blocks = gather_z(residual_far)
    (total,) = kernel_call(
        functools.partial(own_backward_body, pair, scales),
        [stack_f32],
        (*blocks, x1, act, slope, hidden, down, weights),
        4 * product,
        LIMIT,
        grad_scratch,
    )
    far, act, slope, hidden = kernel_call(
        functools.partial(far_forward_body, scale_model),
        [stack_bf16, *acts],
        (core, x1_far, direct, passed),
        2 * product,
        LIMIT,
        (),
        [SMEM_SPEC] + [VMEM_SPEC] * 3,
    )
    return kernel_call(
        functools.partial(last_body, pair, scales),
        [arr((1, units, width), F32)] * 3,
        (*far_blocks, x1_far, act, slope, hidden, far, total),
        4 * product,
        LIMIT,
        (
            pltpu.VMEM((3, units, width), F32),
            pltpu.SemaphoreType.DMA((3,)),
            *grad_scratch,
        ),
        None,
        [pl.BlockSpec(memory_space=pl.ANY)] * 3,
    )


def solution(mesh):
    n_rep, n_hid = mesh.shape["rep"], mesh.shape["hid"]
    hid_spec = P("rep", "hid", None)
    token_spec = P(None, ("rep", "hid"), None)

    def whole(tokens, targets, w_gate, w_up, w_down):
        def body(*args):
            return local(*args, n_rep=n_rep, n_z=n_hid // 2, hidden_units=w_gate.shape[1])

        return jax.shard_map(
            body,
            mesh=mesh,
            in_specs=(token_spec, token_spec, hid_spec, hid_spec, hid_spec),
            out_specs=(hid_spec, hid_spec, hid_spec),
            check_vma=False,
        )(tokens, targets, w_gate, w_up, w_down)

    return whole
```
